256 devices in a mesh: pix: 64 (over x, z, core), band: 4 (over y).
Axes of the slice: x: 4, y: 4, z: 8, core: 2. Of those that a mesh axis runs over, the one named last changes fastest.
Arguments:
- spectra: bfloat16 [224, 262144], P('band', 'pix'), may hold values from -0.1 to 4
- endmembers: bfloat16 [224, 512], P('band'), may hold values from 0.05 to 1
- gram_inverse: float32 [512, 512], replicated, may hold values from -1 to 1, as said below
- abundances: float32 [512, 262144], P(None, ('pix', 'band')), may hold values from 0 to 512, as said below
- duals: float32 [512, 262144], P(None, ('pix', 'band')), may hold values from -4 to 4
Outputs:
- abundances_out: float32 [512, 262144], P(None, ('pix', 'band'))
- duals_out: float32 [512, 262144], P(None, ('pix', 'band'))
- residual_rms: float32 [2, 2], replicated
The draws below stay inside these ranges and needn't reach their ends.
Inputs may be any that keep to these rules, and one draw needn't show every extreme that they name: `abundances`: each column is nonnegative and sums to 512. `gram_inverse`: penalty times the float32 inverse of endmembers^T endmembers / 512^2 + penalty I, with penalty = 224 / (2 * 512^2) and the endmembers as stored.
All inputs are finite; a program needn't handle non-finite values.
Results may differ from the reference program's by a relative error of at most 0.0004.
Values may be sent and summed in bfloat16 or wider, within the bound.
A program may use at most 64 MiB of HBM per device.

```python
import jax
import jax.numpy as jnp
from jax import lax

B = 224
K = 512
ITERS = 2
BISECT = 6
PIXELS = 262144


def endmember_table(key):
    return jax.random.uniform(jax.random.fold_in(key, 11), (B, K), jnp.float32, 0.05, 1.0).astype(jnp.bfloat16)


def draw_endmembers(key, part):
    return endmember_table(key)


def draw_gram_inverse(key, part):
    signatures = endmember_table(key).astype(jnp.float32)
    penalty = B / (2.0 * K * K)
    gram = jnp.dot(signatures.T, signatures, precision=lax.Precision.HIGHEST) / (K * K)
    return penalty * jnp.linalg.inv(gram + penalty * jnp.eye(K, dtype=jnp.float32))


def draw_spectra(key, part):
    signatures = endmember_table(key).astype(jnp.float32)
    logits = 2.0 * jax.random.normal(jax.random.fold_in(key, 21), (K, PIXELS), jnp.float32)
    mixing = K * jax.nn.softmax(logits, axis=0)
    position = jnp.arange(PIXELS, dtype=jnp.float32) / PIXELS
    bright = 0.6 * jnp.power(3.0, position)
    noise = jnp.clip(0.02 * jax.random.normal(jax.random.fold_in(key, 22), (B, PIXELS), jnp.float32), -0.1, 0.1)
    mixed = jnp.dot(signatures, mixing, precision=lax.Precision.HIGHEST) / K
    return (bright[None, :] * mixed + noise).astype(jnp.bfloat16)


def draw_abundances(key, part):
    logits = 1.5 * jax.random.normal(jax.random.fold_in(key, 31), (K, PIXELS), jnp.float32)
    return K * jax.nn.softmax(logits, axis=0)


def draw_duals(key, part):
    position = jnp.arange(PIXELS, dtype=jnp.float32) / PIXELS
    values = jnp.clip(jax.random.normal(jax.random.fold_in(key, 41), (K, PIXELS), jnp.float32), -4.0, 4.0)
    return 0.3 * jnp.power(3.0, position)[None, :] * values


def setup_inputs(seed: int = 0) -> dict:
    seeds = jax.random.split(jax.random.key(seed), 6)
    spectra = draw_spectra(jax.random.fold_in(seeds[5], 71), 0)
    endmembers = draw_endmembers(jax.random.fold_in(seeds[5], 71), 0)
    gram_inverse = draw_gram_inverse(jax.random.fold_in(seeds[5], 71), 0)
    abundances = draw_abundances(jax.random.fold_in(seeds[5], 71), 0)
    duals = draw_duals(jax.random.fold_in(seeds[5], 71), 0)
    return {"spectra": spectra, "endmembers": endmembers, "gram_inverse": gram_inverse, "abundances": abundances, "duals": duals}


def project(shifted):
    simplex_sum = float(K)
    high_end = lax.optimization_barrier(jnp.max(shifted, axis=0))
    low_end = (lax.optimization_barrier(jnp.sum(shifted, axis=0)) - simplex_sum) / simplex_sum

    def mass_at(level):
        return lax.optimization_barrier(jnp.sum(jnp.maximum(shifted - level[None, :], 0.0), axis=0))
    mass_low = mass_at(low_end)
    mass_high = jnp.zeros_like(high_end)

    def bisect_once(unused, state):
        low_now, high_now, low_mass, high_mass = state
        middle = 0.5 * (low_now + high_now)
        total_mass = mass_at(middle)
        too_high = total_mass > simplex_sum
        return (jnp.where(too_high, middle, low_now), jnp.where(too_high, high_now, middle), jnp.where(too_high, total_mass, low_mass), jnp.where(too_high, high_mass, total_mass))
    low_end, high_end, mass_low, mass_high = lax.fori_loop(0, BISECT, bisect_once, (low_end, high_end, mass_low, mass_high))
    level = low_end + (mass_low - simplex_sum) * (high_end - low_end) / (mass_low - mass_high)
    return jnp.maximum(shifted - level[None, :], 0.0)

def reference(spectra, endmembers, gram_inverse, abundances, duals):
    penalty = B / (2.0 * K * K)
    fit_term = jnp.dot(endmembers.T.astype(jnp.float32), spectra.astype(jnp.float32), preferred_element_type=jnp.float32) / K
    current = abundances
    scaled_dual = duals
    primal_list = []
    change_list = []
    for sweep in range(ITERS):
        primal = jnp.dot(gram_inverse, fit_term / penalty + current - scaled_dual, precision=lax.Precision.HIGHEST)
        updated = project(primal + scaled_dual)
        scaled_dual = scaled_dual + primal - updated
        primal_list.append(jnp.sum((primal - updated) ** 2))
        change_list.append(jnp.sum((updated - current) ** 2))
        current = updated
    totals = jnp.stack([jnp.stack(primal_list), jnp.stack(change_list)])
    residual_rms = jnp.sqrt(totals / PIXELS)
    return (current, scaled_dual, residual_rms)
```

```python
import functools

import jax
import jax.numpy as jnp
from jax import lax
from jax.experimental import pallas as pl
from jax.experimental.pallas import tpu as pltpu
from jax.sharding import PartitionSpec as P

K = 512
BISECT = 6
MESH = pl.DeviceIdType.MESH
F32 = jnp.float32
BF16 = jnp.bfloat16
CHUNK = 256


def mxu(a, b):
    return jnp.dot(a, b, preferred_element_type=F32)


def split(value):
    high = value.astype(BF16)
    return high, (value - high.astype(F32)).astype(BF16)


def gather_kernel(bands, padded, scale, spectra, endmembers, gram, y_out, e_out, m_high, m_low,
                  e_send, e_recv, y_send, y_recv, own_sem):
    me = lax.axis_index("band")
    rows = spectra.shape[0]
    columns = y_out.shape[1]
    mine = pl.ds(pl.multiple_of(me * padded, padded), rows)

    own_e = pltpu.make_async_copy(endmembers, e_out.at[mine, :], own_sem.at[0])
    own_y = pltpu.make_async_copy(
        spectra.at[:, pl.ds(pl.multiple_of(me * columns, columns), columns)],
        y_out.at[mine, :], own_sem.at[1])
    barrier = pltpu.get_barrier_semaphore()
    for step in range(1, bands):
        pl.semaphore_signal(barrier, inc=1, device_id={"band": lax.rem(me + step, bands)},
                            device_id_type=MESH)
    if padded > rows:
        for band in range(bands):
            start = band * padded + rows
            y_out[start:start + padded - rows, :] = jnp.zeros((padded - rows, columns), BF16)
            e_out[start:start + padded - rows, :] = jnp.zeros((padded - rows, K), BF16)
    own_e.start()
    own_y.start()
    pl.semaphore_wait(barrier, bands - 1)

    copies_e, copies_y = [], []
    for step in range(1, bands):
        peer = lax.rem(me + step, bands)
        copies_e.append(pltpu.make_async_remote_copy(
            src_ref=endmembers, dst_ref=e_out.at[mine, :],
            send_sem=e_send.at[step - 1], recv_sem=e_recv.at[step - 1],
            device_id={"band": peer}, device_id_type=MESH))
        copies_e[-1].start()
    for step in range(1, bands):
        peer = lax.rem(me + step, bands)
        copies_y.append(pltpu.make_async_remote_copy(
            src_ref=spectra.at[:, pl.ds(pl.multiple_of(peer * columns, columns), columns)],
            dst_ref=y_out.at[mine, :],
            send_sem=y_send.at[step - 1], recv_sem=y_recv.at[step - 1],
            device_id={"band": peer}, device_id_type=MESH))
        copies_y[-1].start()
    own_e.wait()
    for copy in copies_e:
        copy.wait_recv()
    signatures = e_out[...]
    total = jnp.zeros((K, bands * padded), F32)
    rest = gram[...]
    for _ in range(3):
        high = rest.astype(BF16)
        total += lax.dot_general(high, signatures, (((1,), (1,)), ((), ())), preferred_element_type=F32)
        rest = rest - high.astype(F32)
    high, low = split(total * scale)
    m_high[...] = high
    m_low[...] = low
    own_y.wait()
    for copy in copies_y:
        copy.wait_recv()
    for copy in copies_e + copies_y:
        copy.wait_send()


def mass(shifted, level):
    return jnp.sum(jnp.maximum(shifted, level), axis=0, keepdims=True) - K * level


def find_level(shifted):
    high = jnp.max(shifted, axis=0, keepdims=True)
    low = (jnp.sum(shifted, axis=0, keepdims=True) - K) / K
    mass_low = mass(shifted, low)
    mass_high = jnp.zeros_like(high)
    for _ in range(BISECT):
        middle = 0.5 * (low + high)
        total = mass(shifted, middle)
        above = total > K
        low = jnp.where(above, middle, low)
        high = jnp.where(above, high, middle)
        mass_low = jnp.where(above, total, mass_low)
        mass_high = jnp.where(above, mass_high, total)
    return low + (mass_low - K) * (high - low) / (mass_low - mass_high)


def admm_kernel(y_ref, e_ref, mh_ref, ml_ref, z_ref, u_ref, z_out, u_out, sums):
    step = pl.program_id(0)
    current, dual = z_ref[...], u_ref[...]
    spectra = y_ref[...].astype(F32)
    signatures, m_high, m_low = e_ref[...], mh_ref[...], ml_ref[...]
    parts = []
    for sweep in range(2):
        high, low = split(current - dual)
        rest = spectra - (mxu(signatures, high) + mxu(signatures, low)) * (1.0 / K)
        high, low = split(rest)
        shifted = current + (mxu(m_high, high) + mxu(m_low, high) + mxu(m_high, low))
        level = find_level(shifted)
        updated = jnp.maximum(shifted - level, 0.0)
        new_dual = jnp.minimum(shifted, level)
        parts.append(jnp.sum((new_dual - dual) ** 2, axis=0, keepdims=True))
        parts.append(jnp.sum((updated - current) ** 2, axis=0, keepdims=True))
        current, dual = updated, new_dual
    z_out[...] = current
    u_out[...] = dual

    @pl.when(step == 0)
    def _():
        sums[...] = jnp.zeros_like(sums)
    lane = lax.broadcasted_iota(jnp.int32, (1, 128), 1)
    row = jnp.zeros((1, 128), F32)
    for place, part in enumerate((parts[0], parts[2], parts[1], parts[3])):
        row = row + jnp.where(lane == place, jnp.sum(part, axis=1, keepdims=True), 0.0)
    sums[...] += row


def reduce_kernel(bands, sums, out, first, second, mid, send1, recv1, send2, recv2):
    pix, band = lax.axis_index("pix"), lax.axis_index("band")
    inner, outer = 16, 4
    low, x = lax.rem(pix, inner), pix // inner
    place = x * bands + band
    barrier = pltpu.get_barrier_semaphore()

    def target1(step):
        return {"pix": x * inner + lax.rem(low + step, inner), "band": band}

    def target2(step):
        other = lax.rem(place + step, outer * bands)
        return {"pix": (other // bands) * inner + low, "band": lax.rem(other, bands)}

    for step in range(1, inner):
        pl.semaphore_signal(barrier, inc=1, device_id=target1(step), device_id_type=MESH)
    for step in range(1, outer * bands):
        pl.semaphore_signal(barrier, inc=1, device_id=target2(step), device_id_type=MESH)
    first[0] = sums[...]
    pl.semaphore_wait(barrier, inner - 1 + outer * bands - 1)
    copies1, copies2 = [], []
    for step in range(1, inner):
        copies1.append(pltpu.make_async_remote_copy(
            src_ref=sums, dst_ref=first.at[step], send_sem=send1.at[step], recv_sem=recv1.at[step],
            device_id=target1(step), device_id_type=MESH))
        copies1[-1].start()
    for copy in copies1:
        copy.wait_recv()
    total = jnp.sum(first[...], axis=0)
    mid[...] = total
    second[0] = total
    for step in range(1, outer * bands):
        copies2.append(pltpu.make_async_remote_copy(
            src_ref=mid, dst_ref=second.at[step], send_sem=send2.at[step], recv_sem=recv2.at[step],
            device_id=target2(step), device_id_type=MESH))
        copies2[-1].start()
    for copy in copies2:
        copy.wait_recv()
    out[...] = jnp.sum(second[...], axis=0)
    for copy in copies1 + copies2:
        copy.wait_send()


def body(bands, pixels, total_bands, spectra, endmembers, gram_inverse, abundances, duals):
    rows = spectra.shape[0]
    padded = -(-rows // 64) * 64
    depth = bands * padded
    columns = abundances.shape[1]
    penalty = total_bands / (2.0 * K * K)
    vmem = pl.BlockSpec(memory_space=pltpu.VMEM)
    anywhere = pl.BlockSpec(memory_space=pl.ANY)
    y, e, m_high, m_low = pl.pallas_call(
        functools.partial(gather_kernel, bands, padded, 1.0 / (K * penalty)),
        out_shape=(jax.ShapeDtypeStruct((depth, columns), BF16), jax.ShapeDtypeStruct((depth, K), BF16),
                   jax.ShapeDtypeStruct((K, depth), BF16), jax.ShapeDtypeStruct((K, depth), BF16)),
        in_specs=[anywhere, anywhere, vmem],
        out_specs=(vmem,) * 4,
        scratch_shapes=[pltpu.SemaphoreType.DMA((bands - 1,))] * 4 + [pltpu.SemaphoreType.DMA((2,))],
        compiler_params=pltpu.CompilerParams(collective_id=0, has_side_effects=True),
        name="gather",
    )(spectra, endmembers, gram_inverse)
    whole = lambda i: (0, 0)
    block = lambda i: (0, i)
    z, u, sums = pl.pallas_call(
        admm_kernel,
        grid=(columns // CHUNK,),
        out_shape=(jax.ShapeDtypeStruct((K, columns), F32), jax.ShapeDtypeStruct((K, columns), F32),
                   jax.ShapeDtypeStruct((1, 128), F32)),
        in_specs=[pl.BlockSpec((depth, CHUNK), block), pl.BlockSpec((depth, K), whole),
                  pl.BlockSpec((K, depth), whole), pl.BlockSpec((K, depth), whole),
                  pl.BlockSpec((K, CHUNK), block), pl.BlockSpec((K, CHUNK), block)],
        out_specs=(pl.BlockSpec((K, CHUNK), block), pl.BlockSpec((K, CHUNK), block),
                   pl.BlockSpec((1, 128), whole)),
        name="admm",
    )(y, e, m_high, m_low, abundances, duals)
    n1, n2 = 16, 4 * bands
    totals = pl.pallas_call(
        functools.partial(reduce_kernel, bands),
        out_shape=jax.ShapeDtypeStruct((1, 128), F32),
        in_specs=[vmem],
        out_specs=vmem,
        scratch_shapes=[pltpu.VMEM((n1, 1, 128), F32), pltpu.VMEM((n2, 1, 128), F32), pltpu.VMEM((1, 128), F32),
                        pltpu.SemaphoreType.DMA((n1,)), pltpu.SemaphoreType.DMA((n1,)),
                        pltpu.SemaphoreType.DMA((n2,)), pltpu.SemaphoreType.DMA((n2,))],
        compiler_params=pltpu.CompilerParams(collective_id=1, has_side_effects=True),
        name="reduce",
    )(sums)
    residual_rms = jnp.sqrt(totals[0, :4].reshape(2, 2) / pixels)
    return z, u, residual_rms


def solution(mesh):
    bands = mesh.shape["band"]

    def run(spectra, endmembers, gram_inverse, abundances, duals):
        step = functools.partial(body, bands, abundances.shape[1], spectra.shape[0])
        return jax.shard_map(
            step,
            mesh=mesh,
            in_specs=(P("band", "pix"), P("band", None), P(), P(None, ("pix", "band")), P(None, ("pix", "band"))),
            out_specs=(P(None, ("pix", "band")), P(None, ("pix", "band")), P()),
            check_vma=False,
        )(spectra, endmembers, gram_inverse, abundances, duals)

    return run
```

```python
import functools

import jax
import jax.numpy as jnp
from jax import lax
from jax.experimental import pallas as pl
from jax.experimental.pallas import tpu as pltpu
from jax.sharding import PartitionSpec as P

K = 512
BISECT = 6
MESH = pl.DeviceIdType.MESH
F32 = jnp.float32
BF16 = jnp.bfloat16
SEARCH = 512
INNER, OUTER = 16, 4
VMEM_LIMIT = 24 << 20


def mxu(a, b):
    return jnp.dot(a, b, preferred_element_type=F32)


def split(value):
    high = value.astype(BF16)
    return high, (value - high.astype(F32)).astype(BF16)


def apply_model(m_high, m_low, rest):
    high, low = split(rest)
    return mxu(m_high[...], high) + mxu(m_low[...], high) + mxu(m_high[...], low)


def column_fold(ref, place, change, fold):
    total = None
    for k in range(0, K, 8):
        value = change(ref[k:k + 8, place])
        total = value if total is None else fold(total, value)
    return total


def find_levels(shifted, levels):
    width = shifted.shape[1]
    for start in range(0, width, SEARCH):
        place = slice(start, start + SEARCH)
        same = lambda value: value

        def mass(level):
            wide = jnp.broadcast_to(level, (8, SEARCH))
            total = column_fold(shifted, place, lambda value: jnp.maximum(value, wide), jnp.add)
            return jnp.sum(total, axis=0, keepdims=True) - K * level

        high = jnp.max(column_fold(shifted, place, same, jnp.maximum), axis=0, keepdims=True)
        low = (jnp.sum(column_fold(shifted, place, same, jnp.add), axis=0, keepdims=True) - K) / K
        mass_low = mass(low)
        mass_high = jnp.zeros_like(high)
        for _ in range(BISECT):
            middle = 0.5 * (low + high)
            total = mass(middle)
            above = total > K
            low = jnp.where(above, middle, low)
            high = jnp.where(above, high, middle)
            mass_low = jnp.where(above, total, mass_low)
            mass_high = jnp.where(above, mass_high, total)
        levels[:, place] = low + (mass_low - K) * (high - low) / (mass_low - mass_high)


def lane_row(values):
    lane = lax.broadcasted_iota(jnp.int32, (1, 128), 1)
    row = jnp.zeros((1, 128), F32)
    for place, value in values:
        row = row + jnp.where(lane == place, jnp.sum(value, axis=1, keepdims=True), 0.0)
    return row


def square_sum(a, b):
    difference = a - b
    return jnp.sum(difference * difference, axis=0, keepdims=True)


def first_kernel(bands, padded, scale, spectra, endmembers, gram_hbm, z_hbm, u_hbm,
                 y_out, e_out, m_high, m_low, shifted, levels, sums,
                 gram, z_ref, u_ref, e_send, e_recv, y_send, y_recv, local_sem):
    me = lax.axis_index("band")
    rows = spectra.shape[0]
    columns = y_out.shape[1]
    mine = pl.ds(pl.multiple_of(me * padded, padded), rows)

    def spectra_of(band):
        return spectra.at[:, pl.ds(pl.multiple_of(band * columns, columns), columns)]

    peers = [lax.rem(me + step, bands) for step in range(1, bands)]
    barrier = pltpu.get_barrier_semaphore()
    for peer in peers:
        pl.semaphore_signal(barrier, inc=1, device_id={"band": peer}, device_id_type=MESH)
    own = [pltpu.make_async_copy(endmembers, e_out.at[mine, :], local_sem.at[0]),
           pltpu.make_async_copy(gram_hbm, gram, local_sem.at[1]),
           pltpu.make_async_copy(z_hbm, z_ref, local_sem.at[2]),
           pltpu.make_async_copy(u_hbm, u_ref, local_sem.at[3]),
           pltpu.make_async_copy(spectra_of(me), y_out.at[mine, :], local_sem.at[4])]
    for copy in own:
        copy.start()
    if padded > rows:
        for band in range(bands):
            start = band * padded + rows
            y_out[start:start + padded - rows, :] = jnp.zeros((padded - rows, columns), BF16)
            e_out[start:start + padded - rows, :] = jnp.zeros((padded - rows, K), BF16)
    pl.semaphore_wait(barrier, bands - 1)

    copies_e = [pltpu.make_async_remote_copy(
        src_ref=endmembers, dst_ref=e_out.at[mine, :], send_sem=e_send.at[step], recv_sem=e_recv.at[step],
        device_id={"band": peer}, device_id_type=MESH) for step, peer in enumerate(peers)]
    copies_y = [pltpu.make_async_remote_copy(
        src_ref=spectra_of(peer), dst_ref=y_out.at[mine, :], send_sem=y_send.at[step], recv_sem=y_recv.at[step],
        device_id={"band": peer}, device_id_type=MESH) for step, peer in enumerate(peers)]
    for copy in copies_e + copies_y:
        copy.start()

    for copy in own:
        copy.wait()
    for copy in copies_e:
        copy.wait_recv()
    signatures = e_out[...]
    total = jnp.zeros((K, bands * padded), F32)
    rest = gram[...]
    for _ in range(3):
        high = rest.astype(BF16)
        total += lax.dot_general(high, signatures, (((1,), (1,)), ((), ())), preferred_element_type=F32)
        rest = rest - high.astype(F32)
    m_high[...], m_low[...] = split(total * scale)
    high, low = split(z_ref[...] - u_ref[...])
    modelled = (mxu(signatures, high) + mxu(signatures, low)) * (1.0 / K)

    for copy in copies_y:
        copy.wait_recv()
    shifted[...] = z_ref[...] + apply_model(m_high, m_low, y_out[...].astype(F32) - modelled)
    find_levels(shifted, levels)
    value, level = shifted[...], levels[...]
    primal = square_sum(jnp.minimum(value, level), u_ref[...])
    change = square_sum(jnp.maximum(value - level, 0.0), z_ref[...])
    sums[...] = lane_row([(0, primal), (2, change)])
    for copy in copies_e + copies_y:
        copy.wait_send()


def second_kernel(bands, y_ref, e_ref, m_high, m_low, before, levels_before, sums,
                  shifted, levels, totals,
                  local, first, middle, second, send1, recv1, send2, recv2):
    pix, band = lax.axis_index("pix"), lax.axis_index("band")
    low_index, x = lax.rem(pix, INNER), pix // INNER
    place = x * bands + band

    def outer_target(step):
        other = lax.rem(place + step, OUTER * bands)
        return {"pix": (other // bands) * INNER + low_index, "band": lax.rem(other, bands)}

    targets1 = [{"pix": x * INNER + lax.rem(low_index + step, INNER), "band": band} for step in range(1, INNER)]
    targets2 = [outer_target(step) for step in range(1, OUTER * bands)]
    barrier = pltpu.get_barrier_semaphore()
    for target in targets1 + targets2:
        pl.semaphore_signal(barrier, inc=1, device_id=target, device_id_type=MESH)

    level_before = levels_before[...]
    high, low = split(jnp.abs(before[...] - level_before) - level_before)
    modelled = (mxu(e_ref[...], high) + mxu(e_ref[...], low)) * (1.0 / K)
    rest = y_ref[...].astype(F32) - modelled
    shifted[...] = jnp.maximum(before[...] - level_before, 0.0) + apply_model(m_high, m_low, rest)
    find_levels(shifted, levels)
    value, level, old = shifted[...], levels[...], before[...]
    primal = square_sum(jnp.minimum(value, level), jnp.minimum(old, level_before))
    change = square_sum(jnp.maximum(value - level, 0.0), jnp.maximum(old - level_before, 0.0))
    row = sums[...] + lane_row([(1, primal), (3, change)])
    local[...] = row
    first[0] = row

    pl.semaphore_wait(barrier, len(targets1) + len(targets2))
    copies1 = [pltpu.make_async_remote_copy(
        src_ref=local, dst_ref=first.at[step + 1], send_sem=send1.at[step], recv_sem=recv1.at[step],
        device_id=target, device_id_type=MESH) for step, target in enumerate(targets1)]
    for copy in copies1:
        copy.start()
    for copy in copies1:
        copy.wait_recv()
    row = jnp.sum(first[...], axis=0)
    middle[...] = row
    second[0] = row
    copies2 = [pltpu.make_async_remote_copy(
        src_ref=middle, dst_ref=second.at[step + 1], send_sem=send2.at[step], recv_sem=recv2.at[step],
        device_id=target, device_id_type=MESH) for step, target in enumerate(targets2)]
    for copy in copies2:
        copy.start()
    for copy in copies2:
        copy.wait_recv()
    totals[...] = jnp.sum(second[...], axis=0)
    for copy in copies1 + copies2:
        copy.wait_send()


def last_kernel(pixels, shifted, levels, totals, z_out, u_out, rms):
    level = levels[...]
    z_out[...] = jnp.maximum(shifted[...] - level, 0.0)
    u_out[...] = jnp.minimum(shifted[...], level)
    row = jnp.sqrt(totals[...] / pixels)
    rms[0:1, :] = row[:, 0:2]
    rms[1:2, :] = row[:, 2:4]


def body(bands, pixels, total_bands, spectra, endmembers, gram_inverse, abundances, duals):
    rows = spectra.shape[0]
    padded = -(-rows // 64) * 64
    depth = bands * padded
    columns = abundances.shape[1]
    penalty = total_bands / (2.0 * K * K)
    vmem = pl.BlockSpec(memory_space=pltpu.VMEM)
    hbm = pl.BlockSpec(memory_space=pltpu.HBM)
    shape = jax.ShapeDtypeStruct
    dma = pltpu.SemaphoreType.DMA
    y, e, m_high, m_low, shifted, levels, sums = pl.pallas_call(
        functools.partial(first_kernel, bands, padded, 1.0 / (K * penalty)),
        out_shape=(shape((depth, columns), BF16), shape((depth, K), BF16), shape((K, depth), BF16),
                   shape((K, depth), BF16), shape((K, columns), F32), shape((1, columns), F32), shape((1, 128), F32)),
        in_specs=[hbm] * 5,
        out_specs=(vmem,) * 7,
        scratch_shapes=[pltpu.VMEM((K, K), F32), pltpu.VMEM((K, columns), F32), pltpu.VMEM((K, columns), F32)]
        + [dma((bands - 1,))] * 4 + [dma((5,))],
        compiler_params=pltpu.CompilerParams(collective_id=0, has_side_effects=True, vmem_limit_bytes=VMEM_LIMIT),
        name="first",
    )(*[pltpu.with_memory_space_constraint(array, pltpu.HBM)
        for array in (spectra, endmembers, gram_inverse, abundances, duals)])
    n1, n2 = INNER, OUTER * bands
    shifted, levels, totals = pl.pallas_call(
        functools.partial(second_kernel, bands),
        out_shape=(shape((K, columns), F32), shape((1, columns), F32), shape((1, 128), F32)),
        in_specs=[vmem] * 7,
        out_specs=(vmem,) * 3,
        scratch_shapes=[pltpu.VMEM((1, 128), F32), pltpu.VMEM((n1, 1, 128), F32), pltpu.VMEM((1, 128), F32),
                        pltpu.VMEM((n2, 1, 128), F32), dma((n1,)), dma((n1,)), dma((n2,)), dma((n2,))],
        compiler_params=pltpu.CompilerParams(collective_id=1, has_side_effects=True, vmem_limit_bytes=VMEM_LIMIT),
        name="second",
    )(y, e, m_high, m_low, shifted, levels, sums)
    block = pl.BlockSpec((K // 4, columns), lambda i: (i, 0))
    whole = lambda i: (0, 0)
    return pl.pallas_call(
        functools.partial(last_kernel, pixels),
        grid=(4,),
        out_shape=(shape((K, columns), F32), shape((K, columns), F32), shape((2, 2), F32)),
        in_specs=[block, pl.BlockSpec((1, columns), whole), pl.BlockSpec((1, 128), whole)],
        out_specs=(block, block, pl.BlockSpec((2, 2), whole)),
        compiler_params=pltpu.CompilerParams(vmem_limit_bytes=VMEM_LIMIT),
        name="last",
    )(shifted, levels, totals)


def solution(mesh):
    bands = mesh.shape["band"]

    def run(spectra, endmembers, gram_inverse, abundances, duals):
        step = functools.partial(body, bands, abundances.shape[1], spectra.shape[0])
        return jax.shard_map(
            step,
            mesh=mesh,
            in_specs=(P("band", "pix"), P("band", None), P(), P(None, ("pix", "band")), P(None, ("pix", "band"))),
            out_specs=(P(None, ("pix", "band")), P(None, ("pix", "band")), P()),
            check_vma=False,
        )(spectra, endmembers, gram_inverse, abundances, duals)

    return run
```

```python
import functools

import jax
import jax.numpy as jnp
from jax import lax
from jax.experimental import pallas as pl
from jax.experimental.pallas import tpu as pltpu
from jax.sharding import PartitionSpec as P

K = 512
BISECT = 6
MESH = pl.DeviceIdType.MESH
F32 = jnp.float32
BF16 = jnp.bfloat16
SEARCH = 512
OUTER, LONG = 4, 8
PARTS = 2
VMEM_LIMIT = 24 << 20


def mxu(a, b):
    return jnp.dot(a, b, preferred_element_type=F32)


def split(value):
    high = value.astype(BF16)
    return high, (value - high.astype(F32)).astype(BF16)


def apply_model(m_high, m_low, rest):
    high, low = split(rest)
    return mxu(m_high[...], high) + mxu(m_low[...], high) + mxu(m_high[...], low)


def column_fold(ref, place, change, fold):
    total = None
    for k in range(0, K, 8):
        value = change(ref[k:k + 8, place])
        total = value if total is None else fold(total, value)
    return total


def find_levels(shifted, levels, begin, width):
    for start in range(begin, begin + width, SEARCH):
        place = slice(start, start + SEARCH)
        same = lambda value: value

        def mass(level):
            wide = jnp.broadcast_to(level, (8, SEARCH))
            total = column_fold(shifted, place, lambda value: jnp.maximum(value, wide), jnp.add)
            return jnp.sum(total, axis=0, keepdims=True) - K * level

        high = jnp.max(column_fold(shifted, place, same, jnp.maximum), axis=0, keepdims=True)
        low = (jnp.sum(column_fold(shifted, place, same, jnp.add), axis=0, keepdims=True) - K) / K
        mass_low = mass(low)
        mass_high = jnp.zeros_like(high)
        for _ in range(BISECT):
            middle = 0.5 * (low + high)
            total = mass(middle)
            above = total > K
            low = jnp.where(above, middle, low)
            high = jnp.where(above, high, middle)
            mass_low = jnp.where(above, total, mass_low)
            mass_high = jnp.where(above, mass_high, total)
        levels[:, place] = low + (mass_low - K) * (high - low) / (mass_low - mass_high)


def lane_row(values):
    lane = lax.broadcasted_iota(jnp.int32, (1, 128), 1)
    row = jnp.zeros((1, 128), F32)
    for place, value in values:
        row = row + jnp.where(lane == place, jnp.sum(value), 0.0)
    return row


def first_kernel(bands, padded, scale, spectra, endmembers, gram_hbm, z_hbm, u_hbm,
                 y_out, e_out, m_high, m_low, shifted, levels, sums,
                 gram, z_ref, u_ref, w_high, w_low, modelled, e_send, e_recv, f_send, f_recv, y_send, y_recv, local_sem):
    me, pix = lax.axis_index("band"), lax.axis_index("pix")
    core = lax.rem(pix, 2)
    sibling = {"pix": pix + 1 - 2 * core, "band": me}
    rows = spectra.shape[0]
    columns = y_out.shape[1]
    part = columns // PARTS
    half = pl.ds(pl.multiple_of(core * (K // 2), K // 2), K // 2)

    def rows_of(band):
        return pl.ds(pl.multiple_of(band * padded, padded), rows)

    def spectra_of(band, start, width):
        return spectra.at[:, pl.ds(pl.multiple_of(band * columns + start, 128), width)]

    peers = [lax.rem(me + step, bands) for step in range(1, bands)]
    sources = [lax.rem(me + bands - step, bands) for step in range(1, bands)]
    barrier = pltpu.get_barrier_semaphore()
    for target in [{"pix": pix, "band": peer} for peer in peers] + [sibling]:
        pl.semaphore_signal(barrier, inc=1, device_id=target, device_id_type=MESH)
    own = [pltpu.make_async_copy(z_hbm, z_ref, local_sem.at[0]),
           pltpu.make_async_copy(u_hbm, u_ref, local_sem.at[1]),
           pltpu.make_async_copy(gram_hbm, gram, local_sem.at[2]),
           pltpu.make_async_copy(endmembers, e_out.at[rows_of(me), :], local_sem.at[3]),
           pltpu.make_async_copy(spectra_of(me, 0, columns), y_out.at[rows_of(me), :], local_sem.at[4])]
    for copy in own:
        copy.start()
    if padded > rows:
        for band in range(bands):
            start = band * padded + rows
            y_out[start:start + padded - rows, :] = jnp.zeros((padded - rows, columns), BF16)
            e_out[start:start + padded - rows, :] = jnp.zeros((padded - rows, K), BF16)
    pl.semaphore_wait(barrier, bands)

    copies_e = [pltpu.make_async_remote_copy(
        src_ref=endmembers.at[:, half], dst_ref=e_out.at[rows_of(me), half],
        send_sem=e_send.at[step], recv_sem=e_recv.at[step],
        device_id={"pix": pix, "band": peer}, device_id_type=MESH) for step, peer in enumerate(peers)]
    copies_y = [[pltpu.make_async_remote_copy(
        src_ref=spectra_of(peer, start, part), dst_ref=y_out.at[rows_of(me), start:start + part],
        send_sem=y_send.at[start // part, step], recv_sem=y_recv.at[start // part, step],
        device_id={"pix": pix, "band": peer}, device_id_type=MESH) for step, peer in enumerate(peers)]
        for start in range(0, columns, part)]
    for copy in sum(copies_y, copies_e):
        copy.start()
    copies_f = [pltpu.make_async_remote_copy(
        src_ref=e_out.at[rows_of(source), half], dst_ref=e_out.at[rows_of(source), half],
        send_sem=f_send.at[step], recv_sem=f_recv.at[step],
        device_id=sibling, device_id_type=MESH) for step, source in enumerate(sources)]
    for arrival, copy in zip(copies_e, copies_f):
        arrival.wait_recv()
        copy.start()
    for copy in own:
        copy.wait()
    for k in range(0, K, 64):
        w_high[k:k + 64, :], w_low[k:k + 64, :] = split(z_ref[k:k + 64, :] - u_ref[k:k + 64, :])
    for copy in copies_f:
        copy.wait_recv()

    signatures = e_out[...]
    total = jnp.zeros((K, bands * padded), F32)
    rest = gram[...]
    for _ in range(3):
        high = rest.astype(BF16)
        total += lax.dot_general(high, signatures, (((1,), (1,)), ((), ())), preferred_element_type=F32)
        rest = rest - high.astype(F32)
    m_high[...], m_low[...] = split(total * scale)
    modelled[...] = (mxu(signatures, w_high[...]) + mxu(signatures, w_low[...])) * (1.0 / K)

    values = []
    for index, start in enumerate(range(0, columns, part)):
        for copy in copies_y[index]:
            copy.wait_recv()
        place = slice(start, start + part)
        rest = y_out[:, place].astype(F32) - modelled[:, place]
        shifted[:, place] = z_ref[:, place] + apply_model(m_high, m_low, rest)
        find_levels(shifted, levels, start, part)
        level = jnp.broadcast_to(levels[:, place], (8, part))
        primal, change = jnp.zeros((8, part), F32), jnp.zeros((8, part), F32)
        for k in range(0, K, 8):
            value = shifted[k:k + 8, place]
            primal += jnp.square(jnp.minimum(value, level) - u_ref[k:k + 8, place])
            change += jnp.square(jnp.maximum(value - level, 0.0) - z_ref[k:k + 8, place])
        values += [(0, primal), (2, change)]
    sums[...] = lane_row(values)
    for copy in sum(copies_y, copies_e + copies_f):
        copy.wait_send()


def second_kernel(y_ref, e_ref, m_high, m_low, before, levels_before, sums_before, z_out, u_out, sums,
                  w_high, w_low, shifted, levels):
    columns = before.shape[1]
    level_before = levels_before[...]
    for k in range(0, K, 64):
        w_high[k:k + 64, :], w_low[k:k + 64, :] = split(jnp.abs(before[k:k + 64, :] - level_before) - level_before)
    modelled = (mxu(e_ref[...], w_high[...]) + mxu(e_ref[...], w_low[...])) * (1.0 / K)
    rest = y_ref[...].astype(F32) - modelled
    shifted[...] = jnp.maximum(before[...] - level_before, 0.0) + apply_model(m_high, m_low, rest)
    find_levels(shifted, levels, 0, columns)
    values = []
    for start in range(0, columns, SEARCH):
        place = slice(start, start + SEARCH)
        level = jnp.broadcast_to(levels[:, place], (8, SEARCH))
        old = jnp.broadcast_to(levels_before[:, place], (8, SEARCH))
        primal, change = jnp.zeros((8, SEARCH), F32), jnp.zeros((8, SEARCH), F32)
        for k in range(0, K, 8):
            value, earlier = shifted[k:k + 8, place], before[k:k + 8, place]
            z, u = jnp.maximum(value - level, 0.0), jnp.minimum(value, level)
            z_out[k:k + 8, place] = z
            u_out[k:k + 8, place] = u
            primal += jnp.square(u - jnp.minimum(earlier, old))
            change += jnp.square(z - jnp.maximum(earlier - old, 0.0))
        values += [(1, primal), (3, change)]
    sums[...] = sums_before[...] + lane_row(values)


def ring_distance(step, size):
    return min(step, size - step)


def reduce_kernel(bands, mine, totals, first, middle, second, send1, recv1, send2, recv2):
    pix, band = lax.axis_index("pix"), lax.axis_index("band")
    core, z, x = lax.rem(pix, 2), lax.rem(pix // 2, LONG), pix // (2 * LONG)
    steps1 = sorted(((dz, dc) for dz in range(LONG) for dc in range(2) if dz or dc),
                    key=lambda s: -ring_distance(s[0], LONG) * 2 - s[1])
    steps2 = sorted(((dx, dy) for dx in range(OUTER) for dy in range(bands) if dx or dy),
                    key=lambda s: -ring_distance(s[0], OUTER) - ring_distance(s[1], bands))
    targets1 = [{"pix": (x * LONG + lax.rem(z + dz, LONG)) * 2 + lax.rem(core + dc, 2), "band": band}
                for dz, dc in steps1]
    targets2 = [{"pix": (lax.rem(x + dx, OUTER) * LONG + z) * 2 + core, "band": lax.rem(band + dy, bands)}
                for dx, dy in steps2]
    barrier = pltpu.get_barrier_semaphore()
    for target in targets2 + targets1:
        pl.semaphore_signal(barrier, inc=1, device_id=target, device_id_type=MESH)
    first[0] = mine[...]
    pl.semaphore_wait(barrier, len(targets1) + len(targets2))

    def exchange(source, slots, send, recv, targets):
        for step, target in enumerate(targets):
            pltpu.make_async_remote_copy(src_ref=source, dst_ref=slots.at[step + 1], send_sem=send, recv_sem=recv,
                                         device_id=target, device_id_type=MESH).start()
        filled = slots.at[1:len(targets) + 1]
        pltpu.make_async_copy(filled, filled, recv).wait()

    exchange(mine, first, send1, recv1, targets1)
    row = jnp.sum(first[...], axis=0)
    middle[...] = row
    second[0] = row
    exchange(middle, second, send2, recv2, targets2)
    totals[...] = jnp.sum(second[...], axis=0)
    for slots, send, targets in ((first, send1, targets1), (second, send2, targets2)):
        filled = slots.at[1:len(targets) + 1]
        pltpu.make_async_copy(filled, filled, send).wait()


def last_kernel(pixels, totals, rms):
    row = jnp.sqrt(totals[...] / pixels)
    rms[0:1, :] = row[:, 0:2]
    rms[1:2, :] = row[:, 2:4]


def body(bands, pixels, total_bands, spectra, endmembers, gram_inverse, abundances, duals):
    rows = spectra.shape[0]
    padded = -(-rows // 64) * 64
    depth = bands * padded
    columns = abundances.shape[1]
    penalty = total_bands / (2.0 * K * K)
    vmem = pl.BlockSpec(memory_space=pltpu.VMEM)
    hbm = pl.BlockSpec(memory_space=pltpu.HBM)
    shape = jax.ShapeDtypeStruct
    dma = pltpu.SemaphoreType.DMA
    square, wide = shape((K, columns), F32), shape((1, columns), F32)
    line = shape((1, 128), F32)
    big = pltpu.VMEM((K, columns), F32)
    packed = pltpu.VMEM((K, columns), BF16)
    y, e, m_high, m_low, shifted, levels, sums = pl.pallas_call(
        functools.partial(first_kernel, bands, padded, 1.0 / (K * penalty)),
        out_shape=(shape((depth, columns), BF16), shape((depth, K), BF16), shape((K, depth), BF16),
                   shape((K, depth), BF16), square, wide, line),
        in_specs=[hbm] * 5,
        out_specs=(vmem,) * 7,
        scratch_shapes=[pltpu.VMEM((K, K), F32), big, big, packed, packed, pltpu.VMEM((depth, columns), F32)]
        + [dma((bands - 1,))] * 4 + [dma((PARTS, bands - 1))] * 2 + [dma((5,))],
        compiler_params=pltpu.CompilerParams(collective_id=0, has_side_effects=True, vmem_limit_bytes=VMEM_LIMIT),
        name="first",
    )(*[pltpu.with_memory_space_constraint(array, pltpu.HBM)
        for array in (spectra, endmembers, gram_inverse, abundances, duals)])
    z, u, sums = pl.pallas_call(
        second_kernel,
        out_shape=(square, square, line),
        in_specs=[vmem] * 7,
        out_specs=(vmem,) * 3,
        scratch_shapes=[packed, packed, big, pltpu.VMEM((1, columns), F32)],
        compiler_params=pltpu.CompilerParams(vmem_limit_bytes=VMEM_LIMIT),
        name="second",
    )(y, e, m_high, m_low, shifted, levels, sums)
    n1, n2 = 2 * LONG, OUTER * bands
    totals = pl.pallas_call(
        functools.partial(reduce_kernel, bands),
        out_shape=line,
        in_specs=[vmem],
        out_specs=vmem,
        scratch_shapes=[pltpu.VMEM((n1, 1, 128), F32), pltpu.VMEM((1, 128), F32), pltpu.VMEM((n2, 1, 128), F32)]
        + [dma] * 4,
        compiler_params=pltpu.CompilerParams(collective_id=1, has_side_effects=True, vmem_limit_bytes=VMEM_LIMIT),
        name="reduce",
    )(sums)
    rms = pl.pallas_call(
        functools.partial(last_kernel, pixels),
        out_shape=shape((2, 2), F32),
        in_specs=[vmem],
        out_specs=vmem,
        compiler_params=pltpu.CompilerParams(vmem_limit_bytes=VMEM_LIMIT),
        name="last",
    )(totals)
    return z, u, rms


def solution(mesh):
    bands = mesh.shape["band"]

    def run(spectra, endmembers, gram_inverse, abundances, duals):
        step = functools.partial(body, bands, abundances.shape[1], spectra.shape[0])
        return jax.shard_map(
            step,
            mesh=mesh,
            in_specs=(P("band", "pix"), P("band", None), P(), P(None, ("pix", "band")), P(None, ("pix", "band"))),
            out_specs=(P(None, ("pix", "band")), P(None, ("pix", "band")), P()),
            check_vma=False,
        )(spectra, endmembers, gram_inverse, abundances, duals)

    return run
```

```python
import functools

import jax
import jax.numpy as jnp
from jax import lax
from jax.experimental import pallas as pl
from jax.experimental.pallas import tpu as pltpu
from jax.sharding import PartitionSpec as P

K = 512
BISECT = 6
MESH = pl.DeviceIdType.MESH
F32 = jnp.float32
BF16 = jnp.bfloat16
SEARCH = 512
OUTER, LONG = 4, 8
PARTS = 2
VMEM_LIMIT = 24 << 20


def mxu(a, b):
    return jnp.dot(a, b, preferred_element_type=F32)


def split(value):
    high = value.astype(BF16)
    return high, (value - high.astype(F32)).astype(BF16)


def apply_model(m_high, m_low, rest):
    high, low = split(rest)
    return mxu(m_high[...], high) + mxu(m_low[...], high) + mxu(m_high[...], low)


def column_fold(ref, place, change, fold):
    total = None
    for k in range(0, K, 8):
        value = change(ref[k:k + 8, place])
        total = value if total is None else fold(total, value)
    return total


def find_levels(shifted, levels, begin, width):
    for start in range(begin, begin + width, SEARCH):
        place = slice(start, start + SEARCH)
        same = lambda value: value

        def mass(level):
            wide = jnp.broadcast_to(level, (8, SEARCH))
            total = column_fold(shifted, place, lambda value: jnp.maximum(value, wide), jnp.add)
            return jnp.sum(total, axis=0, keepdims=True) - K * level

        high = jnp.max(column_fold(shifted, place, same, jnp.maximum), axis=0, keepdims=True)
        low = (jnp.sum(column_fold(shifted, place, same, jnp.add), axis=0, keepdims=True) - K) / K
        mass_low = mass(low)
        mass_high = jnp.zeros_like(high)
        for _ in range(BISECT):
            middle = 0.5 * (low + high)
            total = mass(middle)
            above = total > K
            low = jnp.where(above, middle, low)
            high = jnp.where(above, high, middle)
            mass_low = jnp.where(above, total, mass_low)
            mass_high = jnp.where(above, mass_high, total)
        levels[:, place] = low + (mass_low - K) * (high - low) / (mass_low - mass_high)


def lane_row(values):
    lane = lax.broadcasted_iota(jnp.int32, (1, 128), 1)
    row = jnp.zeros((1, 128), F32)
    for place, value in values:
        row = row + jnp.where(lane == place, jnp.sum(value), 0.0)
    return row


def first_kernel(bands, padded, scale, spectra, endmembers, gram_hbm, z_hbm, u_hbm,
                 y_out, e_out, m_high, m_low, shifted, levels, sums,
                 gram, z_ref, u_ref, w_high, w_low, e_send, e_recv, f_send, f_recv, y_send, y_recv, local_sem):
    me, pix = lax.axis_index("band"), lax.axis_index("pix")
    core = lax.rem(pix, 2)
    sibling = {"pix": pix + 1 - 2 * core, "band": me}
    rows = spectra.shape[0]
    columns = y_out.shape[1]
    part = columns // PARTS
    half = pl.ds(pl.multiple_of(core * (K // 2), K // 2), K // 2)

    def rows_of(band):
        return pl.ds(pl.multiple_of(band * padded, padded), rows)

    def spectra_of(band, start, width):
        return spectra.at[:, pl.ds(pl.multiple_of(band * columns + start, 128), width)]

    peers = [lax.rem(me + step, bands) for step in range(1, bands)]
    sources = [lax.rem(me + bands - step, bands) for step in range(1, bands)]
    barrier = pltpu.get_barrier_semaphore()
    for target in [{"pix": pix, "band": peer} for peer in peers] + [sibling]:
        pl.semaphore_signal(barrier, inc=1, device_id=target, device_id_type=MESH)
    own = [pltpu.make_async_copy(z_hbm, z_ref, local_sem.at[0]),
           pltpu.make_async_copy(u_hbm, u_ref, local_sem.at[1]),
           pltpu.make_async_copy(gram_hbm, gram, local_sem.at[2]),
           pltpu.make_async_copy(endmembers, e_out.at[rows_of(me), :], local_sem.at[3]),
           pltpu.make_async_copy(spectra_of(me, 0, columns), y_out.at[rows_of(me), :], local_sem.at[4])]
    for copy in own:
        copy.start()
    if padded > rows:
        for band in range(bands):
            start = band * padded + rows
            y_out[start:start + padded - rows, :] = jnp.zeros((padded - rows, columns), BF16)
            e_out[start:start + padded - rows, :] = jnp.zeros((padded - rows, K), BF16)
    pl.semaphore_wait(barrier, bands)

    copies_e = [pltpu.make_async_remote_copy(
        src_ref=endmembers.at[:, half], dst_ref=e_out.at[rows_of(me), half],
        send_sem=e_send.at[step], recv_sem=e_recv.at[step],
        device_id={"pix": pix, "band": peer}, device_id_type=MESH) for step, peer in enumerate(peers)]
    copies_y = [[pltpu.make_async_remote_copy(
        src_ref=spectra_of(peer, start, part), dst_ref=y_out.at[rows_of(me), start:start + part],
        send_sem=y_send.at[start // part, step], recv_sem=y_recv.at[start // part, step],
        device_id={"pix": pix, "band": peer}, device_id_type=MESH) for step, peer in enumerate(peers)]
        for start in range(0, columns, part)]
    for copy in sum(copies_y, copies_e):
        copy.start()
    copies_f = [pltpu.make_async_remote_copy(
        src_ref=e_out.at[rows_of(source), half], dst_ref=e_out.at[rows_of(source), half],
        send_sem=f_send.at[step], recv_sem=f_recv.at[step],
        device_id=sibling, device_id_type=MESH) for step, source in enumerate(sources)]
    for copy in own:
        copy.wait()
    for k in range(0, K, 64):
        w_high[k:k + 64, :], w_low[k:k + 64, :] = split(z_ref[k:k + 64, :] - u_ref[k:k + 64, :])
    g_high, g_low = split(gram[...])
    for start in range(0, columns, part):
        place = slice(start, start + part)
        high = w_high[:, place]
        shifted[:, place] = u_ref[:, place] + (mxu(g_high, high) + mxu(g_low, high) + mxu(g_high, w_low[:, place]))
    for arrival, copy in zip(copies_e, copies_f):
        arrival.wait_recv()
        copy.start()
    for copy in copies_f:
        copy.wait_recv()

    signatures = e_out[...]
    total = jnp.zeros((K, bands * padded), F32)
    rest = gram[...]
    for _ in range(3):
        high = rest.astype(BF16)
        total += lax.dot_general(high, signatures, (((1,), (1,)), ((), ())), preferred_element_type=F32)
        rest = rest - high.astype(F32)
    m_high[...], m_low[...] = split(total * scale)

    values = []
    for index, start in enumerate(range(0, columns, part)):
        for copy in copies_y[index]:
            copy.wait_recv()
        place = slice(start, start + part)
        arrived = y_out[:, place]
        shifted[:, place] += mxu(m_high[...], arrived) + mxu(m_low[...], arrived)
        find_levels(shifted, levels, start, part)
        level = jnp.broadcast_to(levels[:, place], (8, part))
        primal, change = jnp.zeros((8, part), F32), jnp.zeros((8, part), F32)
        for k in range(0, K, 8):
            value = shifted[k:k + 8, place]
            primal += jnp.square(jnp.minimum(value, level) - u_ref[k:k + 8, place])
            change += jnp.square(jnp.maximum(value - level, 0.0) - z_ref[k:k + 8, place])
        values += [(0, primal), (2, change)]
    sums[...] = lane_row(values)
    for copy in sum(copies_y, copies_e + copies_f):
        copy.wait_send()


def second_kernel(y_ref, e_ref, m_high, m_low, before, levels_before, sums_before, z_hbm, u_hbm, sums,
                  w_high, w_low, shifted, levels, z_out, u_out, out_sem):
    columns = before.shape[1]
    level_before = levels_before[...]
    for k in range(0, K, 64):
        w_high[k:k + 64, :], w_low[k:k + 64, :] = split(jnp.abs(before[k:k + 64, :] - level_before) - level_before)
    modelled = (mxu(e_ref[...], w_high[...]) + mxu(e_ref[...], w_low[...])) * (1.0 / K)
    rest = y_ref[...].astype(F32) - modelled
    shifted[...] = jnp.maximum(before[...] - level_before, 0.0) + apply_model(m_high, m_low, rest)
    values, copies = [], []
    for index, start in enumerate(range(0, columns, SEARCH)):
        find_levels(shifted, levels, start, SEARCH)
        place = slice(start, start + SEARCH)
        level = jnp.broadcast_to(levels[:, place], (8, SEARCH))
        old = jnp.broadcast_to(levels_before[:, place], (8, SEARCH))
        primal, change = jnp.zeros((8, SEARCH), F32), jnp.zeros((8, SEARCH), F32)
        for k in range(0, K, 8):
            value, earlier = shifted[k:k + 8, place], before[k:k + 8, place]
            z, u = jnp.maximum(value - level, 0.0), jnp.minimum(value, level)
            z_out[k:k + 8, place] = z
            u_out[k:k + 8, place] = u
            primal += jnp.square(u - jnp.minimum(earlier, old))
            change += jnp.square(z - jnp.maximum(earlier - old, 0.0))
        values += [(1, primal), (3, change)]
        for which, (source, target) in enumerate(((z_out, z_hbm), (u_out, u_hbm))):
            copies.append(pltpu.make_async_copy(source.at[:, place], target.at[:, place], out_sem.at[index, which]))
            copies[-1].start()
    sums[...] = sums_before[...] + lane_row(values)
    for copy in copies:
        copy.wait()


def ring_distance(step, size):
    return min(step, size - step)


def reduce_kernel(bands, mine, totals, first, middle, second, send1, recv1, send2, recv2):
    pix, band = lax.axis_index("pix"), lax.axis_index("band")
    core, z, x = lax.rem(pix, 2), lax.rem(pix // 2, LONG), pix // (2 * LONG)
    steps1 = sorted(((dz, dc) for dz in range(LONG) for dc in range(2) if dz or dc),
                    key=lambda s: -ring_distance(s[0], LONG) * 2 - s[1])
    steps2 = sorted(((dx, dy) for dx in range(OUTER) for dy in range(bands) if dx or dy),
                    key=lambda s: -ring_distance(s[0], OUTER) - ring_distance(s[1], bands))
    targets1 = [{"pix": (x * LONG + lax.rem(z + dz, LONG)) * 2 + lax.rem(core + dc, 2), "band": band}
                for dz, dc in steps1]
    targets2 = [{"pix": (lax.rem(x + dx, OUTER) * LONG + z) * 2 + core, "band": lax.rem(band + dy, bands)}
                for dx, dy in steps2]
    barrier = pltpu.get_barrier_semaphore()
    for target in targets2 + targets1:
        pl.semaphore_signal(barrier, inc=1, device_id=target, device_id_type=MESH)
    first[0] = mine[...]
    pl.semaphore_wait(barrier, len(targets1) + len(targets2))

    def exchange(source, slots, send, recv, targets):
        for step, target in enumerate(targets):
            pltpu.make_async_remote_copy(src_ref=source, dst_ref=slots.at[step + 1], send_sem=send, recv_sem=recv,
                                         device_id=target, device_id_type=MESH).start()
        filled = slots.at[1:len(targets) + 1]
        pltpu.make_async_copy(filled, filled, recv).wait()

    exchange(mine, first, send1, recv1, targets1)
    row = jnp.sum(first[...], axis=0)
    middle[...] = row
    second[0] = row
    exchange(middle, second, send2, recv2, targets2)
    totals[...] = jnp.sum(second[...], axis=0)
    for slots, send, targets in ((first, send1, targets1), (second, send2, targets2)):
        filled = slots.at[1:len(targets) + 1]
        pltpu.make_async_copy(filled, filled, send).wait()


def last_kernel(pixels, totals, rms):
    row = jnp.sqrt(totals[...] / pixels)
    rms[0:1, :] = row[:, 0:2]
    rms[1:2, :] = row[:, 2:4]


def body(bands, pixels, total_bands, spectra, endmembers, gram_inverse, abundances, duals):
    rows = spectra.shape[0]
    padded = -(-rows // 64) * 64
    depth = bands * padded
    columns = abundances.shape[1]
    penalty = total_bands / (2.0 * K * K)
    vmem = pl.BlockSpec(memory_space=pltpu.VMEM)
    hbm = pl.BlockSpec(memory_space=pltpu.HBM)
    shape = jax.ShapeDtypeStruct
    dma = pltpu.SemaphoreType.DMA
    square, wide = shape((K, columns), F32), shape((1, columns), F32)
    line = shape((1, 128), F32)
    big = pltpu.VMEM((K, columns), F32)
    packed = pltpu.VMEM((K, columns), BF16)
    y, e, m_high, m_low, shifted, levels, sums = pl.pallas_call(
        functools.partial(first_kernel, bands, padded, 1.0 / (K * penalty)),
        out_shape=(shape((depth, columns), BF16), shape((depth, K), BF16), shape((K, depth), BF16),
                   shape((K, depth), BF16), square, wide, line),
        in_specs=[hbm] * 5,
        out_specs=(vmem,) * 7,
        scratch_shapes=[pltpu.VMEM((K, K), F32), big, big, packed, packed]
        + [dma((bands - 1,))] * 4 + [dma((PARTS, bands - 1))] * 2 + [dma((5,))],
        compiler_params=pltpu.CompilerParams(collective_id=0, has_side_effects=True, vmem_limit_bytes=VMEM_LIMIT),
        name="first",
    )(*[pltpu.with_memory_space_constraint(array, pltpu.HBM)
        for array in (spectra, endmembers, gram_inverse, abundances, duals)])
    z, u, sums = pl.pallas_call(
        second_kernel,
        out_shape=(square, square, line),
        in_specs=[vmem] * 7,
        out_specs=(hbm, hbm, vmem),
        scratch_shapes=[packed, packed, big, pltpu.VMEM((1, columns), F32), big, big, dma((columns // SEARCH, 2))],
        compiler_params=pltpu.CompilerParams(vmem_limit_bytes=VMEM_LIMIT),
        name="second",
    )(y, e, m_high, m_low, shifted, levels, sums)
    n1, n2 = 2 * LONG, OUTER * bands
    totals = pl.pallas_call(
        functools.partial(reduce_kernel, bands),
        out_shape=line,
        in_specs=[vmem],
        out_specs=vmem,
        scratch_shapes=[pltpu.VMEM((n1, 1, 128), F32), pltpu.VMEM((1, 128), F32), pltpu.VMEM((n2, 1, 128), F32)]
        + [dma] * 4,
        compiler_params=pltpu.CompilerParams(collective_id=1, has_side_effects=True, vmem_limit_bytes=VMEM_LIMIT),
        name="reduce",
    )(sums)
    rms = pl.pallas_call(
        functools.partial(last_kernel, pixels),
        out_shape=shape((2, 2), F32),
        in_specs=[vmem],
        out_specs=vmem,
        compiler_params=pltpu.CompilerParams(vmem_limit_bytes=VMEM_LIMIT),
        name="last",
    )(totals)
    return z, u, rms


def solution(mesh):
    bands = mesh.shape["band"]

    def run(spectra, endmembers, gram_inverse, abundances, duals):
        step = functools.partial(body, bands, abundances.shape[1], spectra.shape[0])
        return jax.shard_map(
            step,
            mesh=mesh,
            in_specs=(P("band", "pix"), P("band", None), P(), P(None, ("pix", "band")), P(None, ("pix", "band"))),
            out_specs=(P(None, ("pix", "band")), P(None, ("pix", "band")), P()),
            check_vma=False,
        )(spectra, endmembers, gram_inverse, abundances, duals)

    return run
```

```python
import functools

import jax
import jax.numpy as jnp
from jax import lax
from jax.experimental import pallas as pl
from jax.experimental.pallas import tpu as pltpu
from jax.sharding import PartitionSpec as P

K = 512
BISECT = 6
MESH = pl.DeviceIdType.MESH
F32 = jnp.float32
BF16 = jnp.bfloat16
SEARCH = 512
OUTER, LONG = 4, 8
OUT_PIECES = 4
PARTS = 2
VMEM_LIMIT = 24 << 20


def mxu(a, b):
    return jnp.dot(a, b, preferred_element_type=F32)


def split(value):
    high = value.astype(BF16)
    return high, (value - high.astype(F32)).astype(BF16)


def apply_model(m_high, m_low, rest):
    high, low = split(rest)
    return mxu(m_high[...], high) + mxu(m_low[...], high) + mxu(m_high[...], low)


def column_fold(ref, place, change, fold):
    total = None
    for k in range(0, K, 8):
        value = change(ref[k:k + 8, place])
        total = value if total is None else fold(total, value)
    return total


def find_levels(shifted, levels, begin, width):
    for start in range(begin, begin + width, SEARCH):
        place = slice(start, start + SEARCH)
        same = lambda value: value

        def mass(level):
            wide = jnp.broadcast_to(level, (8, SEARCH))
            total = column_fold(shifted, place, lambda value: jnp.maximum(value, wide), jnp.add)
            return jnp.sum(total, axis=0, keepdims=True) - K * level

        high = jnp.max(column_fold(shifted, place, same, jnp.maximum), axis=0, keepdims=True)
        low = (jnp.sum(column_fold(shifted, place, same, jnp.add), axis=0, keepdims=True) - K) / K
        mass_low = mass(low)
        mass_high = jnp.zeros_like(high)
        for _ in range(BISECT):
            middle = 0.5 * (low + high)
            total = mass(middle)
            above = total > K
            low = jnp.where(above, middle, low)
            high = jnp.where(above, high, middle)
            mass_low = jnp.where(above, total, mass_low)
            mass_high = jnp.where(above, mass_high, total)
        levels[:, place] = low + (mass_low - K) * (high - low) / (mass_low - mass_high)


def lane_row(values):
    lane = lax.broadcasted_iota(jnp.int32, (1, 128), 1)
    row = jnp.zeros((1, 128), F32)
    for place, value in values:
        row = row + jnp.where(lane == place, jnp.sum(value), 0.0)
    return row


def first_kernel(bands, padded, scale, spectra, endmembers, gram_hbm, z_hbm, u_hbm,
                 y_out, e_out, m_high, m_low, shifted, levels, sums,
                 gram, z_ref, u_ref, w_high, w_low, e_send, e_recv, f_send, f_recv, y_send, y_recv, local_sem):
    me, pix = lax.axis_index("band"), lax.axis_index("pix")
    core = lax.rem(pix, 2)
    sibling = {"pix": pix + 1 - 2 * core, "band": me}
    rows = spectra.shape[0]
    columns = y_out.shape[1]
    part = columns // PARTS
    half = pl.ds(pl.multiple_of(core * (K // 2), K // 2), K // 2)

    def rows_of(band):
        return pl.ds(pl.multiple_of(band * padded, padded), rows)

    def spectra_of(band, start, width):
        return spectra.at[:, pl.ds(pl.multiple_of(band * columns + start, 128), width)]

    peers = [lax.rem(me + step, bands) for step in range(1, bands)]
    sources = [lax.rem(me + bands - step, bands) for step in range(1, bands)]
    barrier = pltpu.get_barrier_semaphore()
    for target in [{"pix": pix, "band": peer} for peer in peers] + [sibling]:
        pl.semaphore_signal(barrier, inc=1, device_id=target, device_id_type=MESH)
    own = [pltpu.make_async_copy(z_hbm, z_ref, local_sem.at[0]),
           pltpu.make_async_copy(u_hbm, u_ref, local_sem.at[1]),
           pltpu.make_async_copy(gram_hbm, gram, local_sem.at[2]),
           pltpu.make_async_copy(endmembers, e_out.at[rows_of(me), :], local_sem.at[3]),
           pltpu.make_async_copy(spectra_of(me, 0, columns), y_out.at[rows_of(me), :], local_sem.at[4])]
    for copy in own:
        copy.start()
    if padded > rows:
        for band in range(bands):
            start = band * padded + rows
            y_out[start:start + padded - rows, :] = jnp.zeros((padded - rows, columns), BF16)
            e_out[start:start + padded - rows, :] = jnp.zeros((padded - rows, K), BF16)
    pl.semaphore_wait(barrier, bands)

    copies_e = [pltpu.make_async_remote_copy(
        src_ref=endmembers.at[:, half], dst_ref=e_out.at[rows_of(me), half],
        send_sem=e_send.at[step], recv_sem=e_recv.at[step],
        device_id={"pix": pix, "band": peer}, device_id_type=MESH) for step, peer in enumerate(peers)]
    copies_y = [[pltpu.make_async_remote_copy(
        src_ref=spectra_of(peer, start, part), dst_ref=y_out.at[rows_of(me), start:start + part],
        send_sem=y_send.at[start // part, step], recv_sem=y_recv.at[start // part, step],
        device_id={"pix": pix, "band": peer}, device_id_type=MESH) for step, peer in enumerate(peers)]
        for start in range(0, columns, part)]
    for copy in sum(copies_y, copies_e):
        copy.start()
    copies_f = [pltpu.make_async_remote_copy(
        src_ref=e_out.at[rows_of(source), half], dst_ref=e_out.at[rows_of(source), half],
        send_sem=f_send.at[step], recv_sem=f_recv.at[step],
        device_id=sibling, device_id_type=MESH) for step, source in enumerate(sources)]
    for copy in own:
        copy.wait()
    for k in range(0, K, 64):
        w_high[k:k + 64, :], w_low[k:k + 64, :] = split(z_ref[k:k + 64, :] - u_ref[k:k + 64, :])
    g_high, g_low = split(gram[...])
    for start in range(0, columns, part):
        place = slice(start, start + part)
        high = w_high[:, place]
        shifted[:, place] = u_ref[:, place] + (mxu(g_high, high) + mxu(g_low, high) + mxu(g_high, w_low[:, place]))
    for arrival, copy in zip(copies_e, copies_f):
        arrival.wait_recv()
        copy.start()
    for copy in copies_f:
        copy.wait_recv()

    signatures = e_out[...]
    total = jnp.zeros((K, bands * padded), F32)
    rest = gram[...]
    for _ in range(3):
        high = rest.astype(BF16)
        total += lax.dot_general(high, signatures, (((1,), (1,)), ((), ())), preferred_element_type=F32)
        rest = rest - high.astype(F32)
    m_high[...], m_low[...] = split(total * scale)

    values = []
    for index, start in enumerate(range(0, columns, part)):
        for copy in copies_y[index]:
            copy.wait_recv()
        place = slice(start, start + part)
        arrived = y_out[:, place]
        shifted[:, place] += mxu(m_high[...], arrived) + mxu(m_low[...], arrived)
        find_levels(shifted, levels, start, part)
        level = jnp.broadcast_to(levels[:, place], (8, part))
        primal, change = jnp.zeros((8, part), F32), jnp.zeros((8, part), F32)
        for k in range(0, K, 8):
            value = shifted[k:k + 8, place]
            primal += jnp.square(jnp.minimum(value, level) - u_ref[k:k + 8, place])
            change += jnp.square(jnp.maximum(value - level, 0.0) - z_ref[k:k + 8, place])
        values += [(0, primal), (2, change)]
    sums[...] = lane_row(values)
    for copy in sum(copies_y, copies_e + copies_f):
        copy.wait_send()


def ring_distance(step, size):
    return min(step, size - step)


def second_kernel(bands, y_ref, e_ref, m_high, m_low, before, levels_before, sums_before, z_out, u_out, totals,
                  w_high, w_low, shifted, levels, mine, first, middle, second, send1, recv1, send2, recv2):
    pix, band = lax.axis_index("pix"), lax.axis_index("band")
    core, z, x = lax.rem(pix, 2), lax.rem(pix // 2, LONG), pix // (2 * LONG)
    steps1 = sorted(((dz, dc) for dz in range(LONG) for dc in range(2) if dz or dc),
                    key=lambda s: -ring_distance(s[0], LONG) * 2 - s[1])
    steps2 = sorted(((dx, dy) for dx in range(OUTER) for dy in range(bands) if dx or dy),
                    key=lambda s: -ring_distance(s[0], OUTER) - ring_distance(s[1], bands))
    targets1 = [{"pix": (x * LONG + lax.rem(z + dz, LONG)) * 2 + lax.rem(core + dc, 2), "band": band}
                for dz, dc in steps1]
    targets2 = [{"pix": (lax.rem(x + dx, OUTER) * LONG + z) * 2 + core, "band": lax.rem(band + dy, bands)}
                for dx, dy in steps2]
    barrier = pltpu.get_barrier_semaphore()
    for target in targets2 + targets1:
        pl.semaphore_signal(barrier, inc=1, device_id=target, device_id_type=MESH)

    columns = before.shape[1]
    level_before = levels_before[...]
    for k in range(0, K, 64):
        w_high[k:k + 64, :], w_low[k:k + 64, :] = split(jnp.abs(before[k:k + 64, :] - level_before) - level_before)
    modelled = (mxu(e_ref[...], w_high[...]) + mxu(e_ref[...], w_low[...])) * (1.0 / K)
    rest = y_ref[...].astype(F32) - modelled
    shifted[...] = jnp.maximum(before[...] - level_before, 0.0) + apply_model(m_high, m_low, rest)
    find_levels(shifted, levels, 0, columns)
    values = []
    for start in range(0, columns, SEARCH):
        place = slice(start, start + SEARCH)
        level = jnp.broadcast_to(levels[:, place], (8, SEARCH))
        old = jnp.broadcast_to(levels_before[:, place], (8, SEARCH))
        primal, change = jnp.zeros((8, SEARCH), F32), jnp.zeros((8, SEARCH), F32)
        for k in range(0, K, 8):
            value, earlier = shifted[k:k + 8, place], before[k:k + 8, place]
            z_new, u_new = jnp.maximum(value - level, 0.0), jnp.minimum(value, level)
            z_out[k:k + 8, place] = z_new
            u_out[k:k + 8, place] = u_new
            primal += jnp.square(u_new - jnp.minimum(earlier, old))
            change += jnp.square(z_new - jnp.maximum(earlier - old, 0.0))
        values += [(1, primal), (3, change)]
    row = sums_before[...] + lane_row(values)
    mine[...] = row
    first[0] = row
    pl.semaphore_wait(barrier, len(targets1) + len(targets2))

    def exchange(source, slots, send, recv, targets):
        for step, target in enumerate(targets):
            pltpu.make_async_remote_copy(src_ref=source, dst_ref=slots.at[step + 1], send_sem=send, recv_sem=recv,
                                         device_id=target, device_id_type=MESH).start()
        filled = slots.at[1:len(targets) + 1]
        pltpu.make_async_copy(filled, filled, recv).wait()

    exchange(mine, first, send1, recv1, targets1)
    row = jnp.sum(first[...], axis=0)
    middle[...] = row
    second[0] = row
    exchange(middle, second, send2, recv2, targets2)
    totals[...] = jnp.sum(second[...], axis=0)
    for slots, send, targets in ((first, send1, targets1), (second, send2, targets2)):
        filled = slots.at[1:len(targets) + 1]
        pltpu.make_async_copy(filled, filled, send).wait()


def last_kernel(pixels, z, u, totals, z_out, u_out, rms, sem):
    copies = []
    for piece in range(OUT_PIECES):
        rows = slice(piece * (K // OUT_PIECES), (piece + 1) * (K // OUT_PIECES))
        for which, (source, target) in enumerate(((z, z_out), (u, u_out))):
            copies.append(pltpu.make_async_copy(source.at[rows, :], target.at[rows, :], sem.at[piece, which]))
            copies[-1].start()
    row = jnp.sqrt(totals[...] / pixels)
    rms[0:1, :] = row[:, 0:2]
    rms[1:2, :] = row[:, 2:4]
    for copy in copies:
        copy.wait()


def body(bands, pixels, total_bands, spectra, endmembers, gram_inverse, abundances, duals):
    rows = spectra.shape[0]
    padded = -(-rows // 64) * 64
    depth = bands * padded
    columns = abundances.shape[1]
    penalty = total_bands / (2.0 * K * K)
    vmem = pl.BlockSpec(memory_space=pltpu.VMEM)
    hbm = pl.BlockSpec(memory_space=pltpu.HBM)
    shape = jax.ShapeDtypeStruct
    dma = pltpu.SemaphoreType.DMA
    square, wide = shape((K, columns), F32), shape((1, columns), F32)
    line = shape((1, 128), F32)
    big = pltpu.VMEM((K, columns), F32)
    packed = pltpu.VMEM((K, columns), BF16)
    y, e, m_high, m_low, shifted, levels, sums = pl.pallas_call(
        functools.partial(first_kernel, bands, padded, 1.0 / (K * penalty)),
        out_shape=(shape((depth, columns), BF16), shape((depth, K), BF16), shape((K, depth), BF16),
                   shape((K, depth), BF16), square, wide, line),
        in_specs=[hbm] * 5,
        out_specs=(vmem,) * 7,
        scratch_shapes=[pltpu.VMEM((K, K), F32), big, big, packed, packed]
        + [dma((bands - 1,))] * 4 + [dma((PARTS, bands - 1))] * 2 + [dma((5,))],
        compiler_params=pltpu.CompilerParams(collective_id=0, has_side_effects=True, vmem_limit_bytes=VMEM_LIMIT),
        name="first",
    )(*[pltpu.with_memory_space_constraint(array, pltpu.HBM)
        for array in (spectra, endmembers, gram_inverse, abundances, duals)])
    n1, n2 = 2 * LONG, OUTER * bands
    resident = pltpu.VMEM((K, columns), F32)
    z, u, totals = pl.pallas_call(
        functools.partial(second_kernel, bands),
        out_shape=(resident, resident, line),
        in_specs=[vmem] * 7,
        out_specs=(vmem,) * 3,
        scratch_shapes=[packed, packed, big, pltpu.VMEM((1, columns), F32), pltpu.VMEM((1, 128), F32),
                        pltpu.VMEM((n1, 1, 128), F32), pltpu.VMEM((1, 128), F32), pltpu.VMEM((n2, 1, 128), F32)]
        + [dma] * 4,
        compiler_params=pltpu.CompilerParams(collective_id=1, has_side_effects=True, vmem_limit_bytes=VMEM_LIMIT),
        name="second",
    )(y, e, m_high, m_low, shifted, levels, sums)
    return pl.pallas_call(
        functools.partial(last_kernel, pixels),
        out_shape=(square, square, shape((2, 2), F32)),
        in_specs=[vmem] * 3,
        out_specs=(hbm, hbm, vmem),
        scratch_shapes=[dma((OUT_PIECES, 2))],
        compiler_params=pltpu.CompilerParams(vmem_limit_bytes=VMEM_LIMIT),
        name="last",
    )(z, u, totals)


def solution(mesh):
    bands = mesh.shape["band"]

    def run(spectra, endmembers, gram_inverse, abundances, duals):
        step = functools.partial(body, bands, abundances.shape[1], spectra.shape[0])
        return jax.shard_map(
            step,
            mesh=mesh,
            in_specs=(P("band", "pix"), P("band", None), P(), P(None, ("pix", "band")), P(None, ("pix", "band"))),
            out_specs=(P(None, ("pix", "band")), P(None, ("pix", "band")), P()),
            check_vma=False,
        )(spectra, endmembers, gram_inverse, abundances, duals)

    return run
```

```python
import functools

import jax
import jax.numpy as jnp
from jax import lax
from jax.experimental import pallas as pl
from jax.experimental.pallas import tpu as pltpu
from jax.sharding import PartitionSpec as P

K = 512
BISECT = 6
MESH = pl.DeviceIdType.MESH
F32 = jnp.float32
BF16 = jnp.bfloat16
SEARCH = 512
OUTER, LONG = 4, 8
OUT_PIECES = 4
EDGES = (0, 5, 8)
VMEM_LIMIT = 24 << 20


def mxu(a, b):
    return jnp.dot(a, b, preferred_element_type=F32)


def split(value):
    high = value.astype(BF16)
    return high, (value - high.astype(F32)).astype(BF16)


def apply_model(m_high, m_low, rest):
    high, low = split(rest)
    return mxu(m_high[...], high) + mxu(m_low[...], high) + mxu(m_high[...], low)


def column_fold(ref, place, change, fold):
    total = None
    for k in range(0, K, 8):
        value = change(ref[k:k + 8, place])
        total = value if total is None else fold(total, value)
    return total


def find_levels(shifted, place):
    width = place.stop - place.start
    same = lambda value: value

    def mass(level):
        wide = jnp.broadcast_to(level, (8, width))
        total = column_fold(shifted, place, lambda value: jnp.maximum(value, wide), jnp.add)
        return jnp.sum(total, axis=0, keepdims=True) - K * level

    high = jnp.max(column_fold(shifted, place, same, jnp.maximum), axis=0, keepdims=True)
    low = (jnp.sum(column_fold(shifted, place, same, jnp.add), axis=0, keepdims=True) - K) / K
    mass_low = mass(low)
    mass_high = jnp.zeros_like(high)
    for _ in range(BISECT):
        middle = 0.5 * (low + high)
        total = mass(middle)
        above = total > K
        low = jnp.where(above, middle, low)
        high = jnp.where(above, high, middle)
        mass_low = jnp.where(above, total, mass_low)
        mass_high = jnp.where(above, mass_high, total)
    return low + (mass_low - K) * (high - low) / (mass_low - mass_high)


def update(shifted, place, z_old, u_old, z_new, u_new):
    width = place.stop - place.start
    level = jnp.broadcast_to(find_levels(shifted, place), (8, width))
    primal, change = jnp.zeros((8, width), F32), jnp.zeros((8, width), F32)
    for k in range(0, K, 8):
        value = shifted[k:k + 8, place]
        z, u = jnp.maximum(value - level, 0.0), jnp.minimum(value, level)
        z_new[k:k + 8, place] = z
        u_new[k:k + 8, place] = u
        primal += jnp.square(u - u_old[k:k + 8, place])
        change += jnp.square(z - z_old[k:k + 8, place])
    return [sum(value[:, start:start + 128] for start in range(0, width, 128)) for value in (primal, change)]


def lane_row(values):
    lane = lax.broadcasted_iota(jnp.int32, (1, 128), 1)
    row = jnp.zeros((1, 128), F32)
    for place, value in enumerate(values):
        total = jnp.sum(jnp.sum(value, axis=0, keepdims=True), axis=1, keepdims=True)
        row = row + jnp.where(lane == place, total, 0.0)
    return row


def first_kernel(bands, padded, scale, spectra, endmembers, gram_hbm, z_hbm, u_hbm,
                 y_out, e_out, m_high, m_low, z_new, u_new, sums,
                 gram, z_ref, u_ref, shifted, w_high, w_low, e_send, e_recv, f_send, f_recv, y_send, y_recv, local_sem):
    me, pix = lax.axis_index("band"), lax.axis_index("pix")
    core = lax.rem(pix, 2)
    sibling = {"pix": pix + 1 - 2 * core, "band": me}
    rows = spectra.shape[0]
    columns = y_out.shape[1]
    edges = [columns * edge // 8 for edge in EDGES]
    parts = list(zip(edges[:-1], edges[1:]))
    half = pl.ds(pl.multiple_of(core * (K // 2), K // 2), K // 2)

    def rows_of(band):
        return pl.ds(pl.multiple_of(band * padded, padded), rows)

    def spectra_of(band, start, width):
        return spectra.at[:, pl.ds(pl.multiple_of(band * columns + start, 128), width)]

    peers = [lax.rem(me + step, bands) for step in range(1, bands)]
    sources = [lax.rem(me + bands - step, bands) for step in range(1, bands)]
    barrier = pltpu.get_barrier_semaphore()
    for target in [{"pix": pix, "band": peer} for peer in peers] + [sibling]:
        pl.semaphore_signal(barrier, inc=1, device_id=target, device_id_type=MESH)
    own = [pltpu.make_async_copy(z_hbm, z_ref, local_sem.at[0]),
           pltpu.make_async_copy(u_hbm, u_ref, local_sem.at[1]),
           pltpu.make_async_copy(gram_hbm, gram, local_sem.at[2]),
           pltpu.make_async_copy(endmembers, e_out.at[rows_of(me), :], local_sem.at[3]),
           pltpu.make_async_copy(spectra_of(me, 0, columns), y_out.at[rows_of(me), :], local_sem.at[4])]
    for copy in own:
        copy.start()
    if padded > rows:
        for band in range(bands):
            start = band * padded + rows
            y_out[start:start + padded - rows, :] = jnp.zeros((padded - rows, columns), BF16)
            e_out[start:start + padded - rows, :] = jnp.zeros((padded - rows, K), BF16)
    pl.semaphore_wait(barrier, bands)

    copies_e = [pltpu.make_async_remote_copy(
        src_ref=endmembers.at[:, half], dst_ref=e_out.at[rows_of(me), half],
        send_sem=e_send.at[step], recv_sem=e_recv.at[step],
        device_id={"pix": pix, "band": peer}, device_id_type=MESH) for step, peer in enumerate(peers)]
    copies_y = [[pltpu.make_async_remote_copy(
        src_ref=spectra_of(peer, start, stop - start), dst_ref=y_out.at[rows_of(me), start:stop],
        send_sem=y_send.at[index, step], recv_sem=y_recv.at[index, step],
        device_id={"pix": pix, "band": peer}, device_id_type=MESH) for step, peer in enumerate(peers)]
        for index, (start, stop) in enumerate(parts)]
    for copy in sum(copies_y, copies_e):
        copy.start()
    copies_f = [pltpu.make_async_remote_copy(
        src_ref=e_out.at[rows_of(source), half], dst_ref=e_out.at[rows_of(source), half],
        send_sem=f_send.at[step], recv_sem=f_recv.at[step],
        device_id=sibling, device_id_type=MESH) for step, source in enumerate(sources)]
    for copy in own:
        copy.wait()
    for k in range(0, K, 64):
        w_high[k:k + 64, :], w_low[k:k + 64, :] = split(z_ref[k:k + 64, :] - u_ref[k:k + 64, :])
    g_high, g_low = split(gram[...])
    for start in range(0, columns, SEARCH):
        place = slice(start, start + SEARCH)
        high = w_high[:, place]
        shifted[:, place] = u_ref[:, place] + (mxu(g_high, high) + mxu(g_low, high) + mxu(g_high, w_low[:, place]))
    for arrival, copy in zip(copies_e, copies_f):
        arrival.wait_recv()
        copy.start()
    for copy in copies_f:
        copy.wait_recv()

    signatures = e_out[...]
    total = jnp.zeros((K, bands * padded), F32)
    rest = gram[...]
    for _ in range(3):
        high = rest.astype(BF16)
        total += lax.dot_general(high, signatures, (((1,), (1,)), ((), ())), preferred_element_type=F32)
        rest = rest - high.astype(F32)
    m_high[...], m_low[...] = split(total * scale)

    values = []
    for arrivals, (start, stop) in zip(copies_y, parts):
        for copy in arrivals:
            copy.wait_recv()
        place = slice(start, stop)
        arrived = y_out[:, place]
        shifted[:, place] += mxu(m_high[...], arrived) + mxu(m_low[...], arrived)
        values.append(update(shifted, place, z_ref, u_ref, z_new, u_new))
    sums[0], sums[1] = (sum(pair[which] for pair in values) for which in range(2))
    for copy in sum(copies_y, copies_e + copies_f):
        copy.wait_send()


def ring_distance(step, size):
    return min(step, size - step)


def second_kernel(bands, y_ref, e_ref, m_high, m_low, z_old, u_old, sums_before, z_out, u_out, totals,
                  w_high, w_low, shifted, mine, first, middle, second, send1, recv1, send2, recv2):
    pix, band = lax.axis_index("pix"), lax.axis_index("band")
    core, z, x = lax.rem(pix, 2), lax.rem(pix // 2, LONG), pix // (2 * LONG)
    steps1 = sorted(((dz, dc) for dz in range(LONG) for dc in range(2) if dz or dc),
                    key=lambda s: -ring_distance(s[0], LONG) * 2 - s[1])
    steps2 = sorted(((dx, dy) for dx in range(OUTER) for dy in range(bands) if dx or dy),
                    key=lambda s: -ring_distance(s[0], OUTER) - ring_distance(s[1], bands))
    targets1 = [{"pix": (x * LONG + lax.rem(z + dz, LONG)) * 2 + lax.rem(core + dc, 2), "band": band}
                for dz, dc in steps1]
    targets2 = [{"pix": (lax.rem(x + dx, OUTER) * LONG + z) * 2 + core, "band": lax.rem(band + dy, bands)}
                for dx, dy in steps2]
    barrier = pltpu.get_barrier_semaphore()
    for target in targets2 + targets1:
        pl.semaphore_signal(barrier, inc=1, device_id=target, device_id_type=MESH)

    columns = z_old.shape[1]
    for k in range(0, K, 64):
        w_high[k:k + 64, :], w_low[k:k + 64, :] = split(z_old[k:k + 64, :] - u_old[k:k + 64, :])
    modelled = (mxu(e_ref[...], w_high[...]) + mxu(e_ref[...], w_low[...])) * (1.0 / K)
    rest = y_ref[...].astype(F32) - modelled
    shifted[...] = z_old[...] + apply_model(m_high, m_low, rest)
    values = [update(shifted, slice(start, start + SEARCH), z_old, u_old, z_out, u_out)
              for start in range(0, columns, SEARCH)]
    primal, change = (sum(pair[which] for pair in values) for which in range(2))
    row = lane_row([sums_before[0], primal, sums_before[1], change])
    mine[...] = row
    first[0] = row
    pl.semaphore_wait(barrier, len(targets1) + len(targets2))

    def exchange(source, slots, send, recv, targets):
        for step, target in enumerate(targets):
            pltpu.make_async_remote_copy(src_ref=source, dst_ref=slots.at[step + 1], send_sem=send, recv_sem=recv,
                                         device_id=target, device_id_type=MESH).start()
        filled = slots.at[1:len(targets) + 1]
        pltpu.make_async_copy(filled, filled, recv).wait()

    exchange(mine, first, send1, recv1, targets1)
    row = jnp.sum(first[...], axis=0)
    middle[...] = row
    second[0] = row
    exchange(middle, second, send2, recv2, targets2)
    totals[...] = jnp.sum(second[...], axis=0)
    for slots, send, targets in ((first, send1, targets1), (second, send2, targets2)):
        filled = slots.at[1:len(targets) + 1]
        pltpu.make_async_copy(filled, filled, send).wait()


def last_kernel(pixels, z, u, totals, z_out, u_out, rms, sem):
    copies = []
    for piece in range(OUT_PIECES):
        rows = slice(piece * (K // OUT_PIECES), (piece + 1) * (K // OUT_PIECES))
        for which, (source, target) in enumerate(((z, z_out), (u, u_out))):
            copies.append(pltpu.make_async_copy(source.at[rows, :], target.at[rows, :], sem.at[piece, which]))
            copies[-1].start()
    row = jnp.sqrt(totals[...] / pixels)
    rms[0:1, :] = row[:, 0:2]
    rms[1:2, :] = row[:, 2:4]
    for copy in copies:
        copy.wait()


def body(bands, pixels, total_bands, spectra, endmembers, gram_inverse, abundances, duals):
    rows = spectra.shape[0]
    padded = -(-rows // 64) * 64
    depth = bands * padded
    columns = abundances.shape[1]
    penalty = total_bands / (2.0 * K * K)
    vmem = pl.BlockSpec(memory_space=pltpu.VMEM)
    hbm = pl.BlockSpec(memory_space=pltpu.HBM)
    shape = jax.ShapeDtypeStruct
    dma = pltpu.SemaphoreType.DMA
    square = shape((K, columns), F32)
    line = shape((1, 128), F32)
    big = pltpu.VMEM((K, columns), F32)
    packed = pltpu.VMEM((K, columns), BF16)
    y, e, m_high, m_low, z, u, sums = pl.pallas_call(
        functools.partial(first_kernel, bands, padded, 1.0 / (K * penalty)),
        out_shape=(shape((depth, columns), BF16), shape((depth, K), BF16), shape((K, depth), BF16),
                   shape((K, depth), BF16), square, square, shape((2, 8, 128), F32)),
        in_specs=[hbm] * 5,
        out_specs=(vmem,) * 7,
        scratch_shapes=[pltpu.VMEM((K, K), F32), big, big, big, packed, packed]
        + [dma((bands - 1,))] * 4 + [dma((len(EDGES) - 1, bands - 1))] * 2 + [dma((5,))],
        compiler_params=pltpu.CompilerParams(collective_id=0, has_side_effects=True, vmem_limit_bytes=VMEM_LIMIT),
        name="first",
    )(*[pltpu.with_memory_space_constraint(array, pltpu.HBM)
        for array in (spectra, endmembers, gram_inverse, abundances, duals)])
    n1, n2 = 2 * LONG, OUTER * bands
    resident = pltpu.VMEM((K, columns), F32)
    z, u, totals = pl.pallas_call(
        functools.partial(second_kernel, bands),
        out_shape=(resident, resident, line),
        in_specs=[vmem] * 7,
        out_specs=(vmem,) * 3,
        scratch_shapes=[packed, packed, big, pltpu.VMEM((1, 128), F32),
                        pltpu.VMEM((n1, 1, 128), F32), pltpu.VMEM((1, 128), F32), pltpu.VMEM((n2, 1, 128), F32)]
        + [dma] * 4,
        compiler_params=pltpu.CompilerParams(collective_id=1, has_side_effects=True, vmem_limit_bytes=VMEM_LIMIT),
        name="second",
    )(y, e, m_high, m_low, z, u, sums)
    return pl.pallas_call(
        functools.partial(last_kernel, pixels),
        out_shape=(square, square, shape((2, 2), F32)),
        in_specs=[vmem] * 3,
        out_specs=(hbm, hbm, vmem),
        scratch_shapes=[dma((OUT_PIECES, 2))],
        compiler_params=pltpu.CompilerParams(vmem_limit_bytes=VMEM_LIMIT),
        name="last",
    )(z, u, totals)


def solution(mesh):
    bands = mesh.shape["band"]

    def run(spectra, endmembers, gram_inverse, abundances, duals):
        step = functools.partial(body, bands, abundances.shape[1], spectra.shape[0])
        return jax.shard_map(
            step,
            mesh=mesh,
            in_specs=(P("band", "pix"), P("band", None), P(), P(None, ("pix", "band")), P(None, ("pix", "band"))),
            out_specs=(P(None, ("pix", "band")), P(None, ("pix", "band")), P()),
            check_vma=False,
        )(spectra, endmembers, gram_inverse, abundances, duals)

    return run
```

```python
import functools

import jax
import jax.numpy as jnp
from jax import lax
from jax.experimental import pallas as pl
from jax.experimental.pallas import tpu as pltpu
from jax.sharding import PartitionSpec as P

K = 512
BISECT = 6
MESH = pl.DeviceIdType.MESH
F32 = jnp.float32
BF16 = jnp.bfloat16
SEARCH = 512
OUTER, LONG = 4, 8
OUT_PIECES = 4
PARTS = 2
VMEM_LIMIT = 24 << 20


def mxu(a, b):
    return jnp.dot(a, b, preferred_element_type=F32)


def split(value):
    high = value.astype(BF16)
    return high, (value - high.astype(F32)).astype(BF16)


def apply_model(m_high, m_low, rest):
    high, low = split(rest)
    return mxu(m_high[...], high) + mxu(m_low[...], high) + mxu(m_high[...], low)


def column_fold(ref, place, change, fold):
    total = None
    for k in range(0, K, 8):
        value = change(ref[k:k + 8, place])
        total = value if total is None else fold(total, value)
    return total


def find_levels(shifted, levels, begin, width):
    for start in range(begin, begin + width, SEARCH):
        place = slice(start, start + SEARCH)
        same = lambda value: value

        def mass(level):
            wide = jnp.broadcast_to(level, (8, SEARCH))
            total = column_fold(shifted, place, lambda value: jnp.maximum(value, wide), jnp.add)
            return jnp.sum(total, axis=0, keepdims=True) - K * level

        high = jnp.max(column_fold(shifted, place, same, jnp.maximum), axis=0, keepdims=True)
        low = (jnp.sum(column_fold(shifted, place, same, jnp.add), axis=0, keepdims=True) - K) / K
        mass_low = mass(low)
        mass_high = jnp.zeros_like(high)
        for _ in range(BISECT):
            middle = 0.5 * (low + high)
            total = mass(middle)
            above = total > K
            low = jnp.where(above, middle, low)
            high = jnp.where(above, high, middle)
            mass_low = jnp.where(above, total, mass_low)
            mass_high = jnp.where(above, mass_high, total)
        levels[:, place] = low + (mass_low - K) * (high - low) / (mass_low - mass_high)


def lane_row(values):
    lane = lax.broadcasted_iota(jnp.int32, (1, 128), 1)
    row = jnp.zeros((1, 128), F32)
    for place, value in values:
        row = row + jnp.where(lane == place, jnp.sum(value, axis=1, keepdims=True), 0.0)
    return row


def fold_lanes(value):
    width = value.shape[1]
    total = sum(value[:, start:start + 128] for start in range(0, width, 128))
    return jnp.sum(total, axis=0, keepdims=True)


def first_kernel(bands, padded, scale, spectra, endmembers, gram_hbm, z_hbm, u_hbm,
                 y_out, e_out, m_high, m_low, shifted, levels, sums,
                 gram, z_ref, u_ref, w_high, w_low, e_send, e_recv, f_send, f_recv, y_send, y_recv, local_sem):
    me, pix = lax.axis_index("band"), lax.axis_index("pix")
    core = lax.rem(pix, 2)
    sibling = {"pix": pix + 1 - 2 * core, "band": me}
    rows = spectra.shape[0]
    columns = y_out.shape[1]
    part = columns // PARTS
    half = pl.ds(pl.multiple_of(core * (K // 2), K // 2), K // 2)

    def rows_of(band):
        return pl.ds(pl.multiple_of(band * padded, padded), rows)

    def spectra_of(band, start, width):
        return spectra.at[:, pl.ds(pl.multiple_of(band * columns + start, 128), width)]

    peers = [lax.rem(me + step, bands) for step in range(1, bands)]
    sources = [lax.rem(me + bands - step, bands) for step in range(1, bands)]
    barrier = pltpu.get_barrier_semaphore()
    for target in [{"pix": pix, "band": peer} for peer in peers] + [sibling]:
        pl.semaphore_signal(barrier, inc=1, device_id=target, device_id_type=MESH)
    own = [pltpu.make_async_copy(z_hbm, z_ref, local_sem.at[0]),
           pltpu.make_async_copy(u_hbm, u_ref, local_sem.at[1]),
           pltpu.make_async_copy(gram_hbm, gram, local_sem.at[2]),
           pltpu.make_async_copy(endmembers, e_out.at[rows_of(me), :], local_sem.at[3]),
           pltpu.make_async_copy(spectra_of(me, 0, columns), y_out.at[rows_of(me), :], local_sem.at[4])]
    for copy in own:
        copy.start()
    if padded > rows:
        for band in range(bands):
            start = band * padded + rows
            y_out[start:start + padded - rows, :] = jnp.zeros((padded - rows, columns), BF16)
            e_out[start:start + padded - rows, :] = jnp.zeros((padded - rows, K), BF16)
    pl.semaphore_wait(barrier, bands)

    copies_e = [pltpu.make_async_remote_copy(
        src_ref=endmembers.at[:, half], dst_ref=e_out.at[rows_of(me), half],
        send_sem=e_send.at[step], recv_sem=e_recv.at[step],
        device_id={"pix": pix, "band": peer}, device_id_type=MESH) for step, peer in enumerate(peers)]
    copies_y = [[pltpu.make_async_remote_copy(
        src_ref=spectra_of(peer, start, part), dst_ref=y_out.at[rows_of(me), start:start + part],
        send_sem=y_send.at[start // part, step], recv_sem=y_recv.at[start // part, step],
        device_id={"pix": pix, "band": peer}, device_id_type=MESH) for step, peer in enumerate(peers)]
        for start in range(0, columns, part)]
    for copy in sum(copies_y, copies_e):
        copy.start()
    copies_f = [pltpu.make_async_remote_copy(
        src_ref=e_out.at[rows_of(source), half], dst_ref=e_out.at[rows_of(source), half],
        send_sem=f_send.at[step], recv_sem=f_recv.at[step],
        device_id=sibling, device_id_type=MESH) for step, source in enumerate(sources)]
    for copy in own:
        copy.wait()
    for k in range(0, K, 64):
        w_high[k:k + 64, :], w_low[k:k + 64, :] = split(z_ref[k:k + 64, :] - u_ref[k:k + 64, :])
    g_high, g_low = split(gram[...])
    for start in range(0, columns, part):
        place = slice(start, start + part)
        high = w_high[:, place]
        shifted[:, place] = u_ref[:, place] + (mxu(g_high, high) + mxu(g_low, high) + mxu(g_high, w_low[:, place]))
    for arrival, copy in zip(copies_e, copies_f):
        arrival.wait_recv()
        copy.start()
    for copy in copies_f:
        copy.wait_recv()

    signatures = e_out[...]
    total = jnp.zeros((K, bands * padded), F32)
    rest = gram[...]
    for _ in range(3):
        high = rest.astype(BF16)
        total += lax.dot_general(high, signatures, (((1,), (1,)), ((), ())), preferred_element_type=F32)
        rest = rest - high.astype(F32)
    m_high[...], m_low[...] = split(total * scale)

    values = []
    for index, start in enumerate(range(0, columns, part)):
        for copy in copies_y[index]:
            copy.wait_recv()
        place = slice(start, start + part)
        arrived = y_out[:, place]
        shifted[:, place] += mxu(m_high[...], arrived) + mxu(m_low[...], arrived)
        find_levels(shifted, levels, start, part)
        level = jnp.broadcast_to(levels[:, place], (8, part))
        primal, change = jnp.zeros((8, part), F32), jnp.zeros((8, part), F32)
        for k in range(0, K, 8):
            value = shifted[k:k + 8, place]
            dual = jnp.minimum(value, level)
            primal += jnp.square(dual - u_ref[k:k + 8, place])
            change += jnp.square(value - dual - z_ref[k:k + 8, place])
        values += [(0, fold_lanes(primal)), (2, fold_lanes(change))]
    sums[...] = lane_row(values)
    for copy in sum(copies_y, copies_e + copies_f):
        copy.wait_send()


def ring_distance(step, size):
    return min(step, size - step)


def second_kernel(bands, y_ref, e_ref, m_high, m_low, before, levels_before, sums_before, z_out, u_out, totals,
                  w_high, w_low, shifted, levels, mine, first, middle, second, send1, recv1, send2, recv2):
    pix, band = lax.axis_index("pix"), lax.axis_index("band")
    core, z, x = lax.rem(pix, 2), lax.rem(pix // 2, LONG), pix // (2 * LONG)
    steps1 = sorted(((dz, dc) for dz in range(LONG) for dc in range(2) if dz or dc),
                    key=lambda s: -ring_distance(s[0], LONG) * 2 - s[1])
    steps2 = sorted(((dx, dy) for dx in range(OUTER) for dy in range(bands) if dx or dy),
                    key=lambda s: -ring_distance(s[0], OUTER) - ring_distance(s[1], bands))
    targets1 = [{"pix": (x * LONG + lax.rem(z + dz, LONG)) * 2 + lax.rem(core + dc, 2), "band": band}
                for dz, dc in steps1]
    targets2 = [{"pix": (lax.rem(x + dx, OUTER) * LONG + z) * 2 + core, "band": lax.rem(band + dy, bands)}
                for dx, dy in steps2]
    barrier = pltpu.get_barrier_semaphore()
    for target in targets2 + targets1:
        pl.semaphore_signal(barrier, inc=1, device_id=target, device_id_type=MESH)

    columns = before.shape[1]
    level_before = levels_before[...]
    for k in range(0, K, 64):
        w_high[k:k + 64, :], w_low[k:k + 64, :] = split(jnp.abs(before[k:k + 64, :] - level_before) - level_before)
    modelled = (mxu(e_ref[...], w_high[...]) + mxu(e_ref[...], w_low[...])) * (1.0 / K)
    rest = y_ref[...].astype(F32) - modelled
    shifted[...] = before[...] - jnp.minimum(before[...], level_before) + apply_model(m_high, m_low, rest)
    find_levels(shifted, levels, 0, columns)
    values = []
    for start in range(0, columns, SEARCH):
        place = slice(start, start + SEARCH)
        level = jnp.broadcast_to(levels[:, place], (8, SEARCH))
        old = jnp.broadcast_to(levels_before[:, place], (8, SEARCH))
        primal, change = jnp.zeros((8, SEARCH), F32), jnp.zeros((8, SEARCH), F32)
        for k in range(0, K, 8):
            value, earlier = shifted[k:k + 8, place], before[k:k + 8, place]
            u_new, u_old = jnp.minimum(value, level), jnp.minimum(earlier, old)
            z_new = value - u_new
            z_out[k:k + 8, place] = z_new
            u_out[k:k + 8, place] = u_new
            primal += jnp.square(u_new - u_old)
            change += jnp.square(z_new - (earlier - u_old))
        values += [(1, fold_lanes(primal)), (3, fold_lanes(change))]
    row = sums_before[...] + lane_row(values)
    mine[...] = row
    first[0] = row
    pl.semaphore_wait(barrier, len(targets1) + len(targets2))

    def exchange(source, slots, send, recv, targets):
        for step, target in enumerate(targets):
            pltpu.make_async_remote_copy(src_ref=source, dst_ref=slots.at[step + 1], send_sem=send, recv_sem=recv,
                                         device_id=target, device_id_type=MESH).start()
        filled = slots.at[1:len(targets) + 1]
        pltpu.make_async_copy(filled, filled, recv).wait()

    exchange(mine, first, send1, recv1, targets1)
    row = jnp.sum(first[...], axis=0)
    middle[...] = row
    second[0] = row
    exchange(middle, second, send2, recv2, targets2)
    totals[...] = jnp.sum(second[...], axis=0)
    for slots, send, targets in ((first, send1, targets1), (second, send2, targets2)):
        filled = slots.at[1:len(targets) + 1]
        pltpu.make_async_copy(filled, filled, send).wait()


def last_kernel(pixels, z, u, totals, z_out, u_out, rms, sem):
    copies = []
    for piece in range(OUT_PIECES):
        rows = slice(piece * (K // OUT_PIECES), (piece + 1) * (K // OUT_PIECES))
        for which, (source, target) in enumerate(((z, z_out), (u, u_out))):
            copies.append(pltpu.make_async_copy(source.at[rows, :], target.at[rows, :], sem.at[piece, which]))
            copies[-1].start()
    row = jnp.sqrt(totals[...] / pixels)
    rms[0:1, :] = row[:, 0:2]
    rms[1:2, :] = row[:, 2:4]
    for copy in copies:
        copy.wait()


def body(bands, pixels, total_bands, spectra, endmembers, gram_inverse, abundances, duals):
    rows = spectra.shape[0]
    padded = -(-rows // 64) * 64
    depth = bands * padded
    columns = abundances.shape[1]
    penalty = total_bands / (2.0 * K * K)
    vmem = pl.BlockSpec(memory_space=pltpu.VMEM)
    hbm = pl.BlockSpec(memory_space=pltpu.HBM)
    shape = jax.ShapeDtypeStruct
    dma = pltpu.SemaphoreType.DMA
    square, wide = shape((K, columns), F32), shape((1, columns), F32)
    line = shape((1, 128), F32)
    big = pltpu.VMEM((K, columns), F32)
    packed = pltpu.VMEM((K, columns), BF16)
    y, e, m_high, m_low, shifted, levels, sums = pl.pallas_call(
        functools.partial(first_kernel, bands, padded, 1.0 / (K * penalty)),
        out_shape=(shape((depth, columns), BF16), shape((depth, K), BF16), shape((K, depth), BF16),
                   shape((K, depth), BF16), square, wide, line),
        in_specs=[hbm] * 5,
        out_specs=(vmem,) * 7,
        scratch_shapes=[pltpu.VMEM((K, K), F32), big, big, packed, packed]
        + [dma((bands - 1,))] * 4 + [dma((PARTS, bands - 1))] * 2 + [dma((5,))],
        compiler_params=pltpu.CompilerParams(collective_id=0, has_side_effects=True, vmem_limit_bytes=VMEM_LIMIT),
        name="first",
    )(*[pltpu.with_memory_space_constraint(array, pltpu.HBM)
        for array in (spectra, endmembers, gram_inverse, abundances, duals)])
    n1, n2 = 2 * LONG, OUTER * bands
    resident = pltpu.VMEM((K, columns), F32)
    z, u, totals = pl.pallas_call(
        functools.partial(second_kernel, bands),
        out_shape=(resident, resident, line),
        in_specs=[vmem] * 7,
        out_specs=(vmem,) * 3,
        scratch_shapes=[packed, packed, big, pltpu.VMEM((1, columns), F32), pltpu.VMEM((1, 128), F32),
                        pltpu.VMEM((n1, 1, 128), F32), pltpu.VMEM((1, 128), F32), pltpu.VMEM((n2, 1, 128), F32)]
        + [dma] * 4,
        compiler_params=pltpu.CompilerParams(collective_id=1, has_side_effects=True, vmem_limit_bytes=VMEM_LIMIT),
        name="second",
    )(y, e, m_high, m_low, shifted, levels, sums)
    return pl.pallas_call(
        functools.partial(last_kernel, pixels),
        out_shape=(square, square, shape((2, 2), F32)),
        in_specs=[vmem] * 3,
        out_specs=(hbm, hbm, vmem),
        scratch_shapes=[dma((OUT_PIECES, 2))],
        compiler_params=pltpu.CompilerParams(vmem_limit_bytes=VMEM_LIMIT),
        name="last",
    )(z, u, totals)


def solution(mesh):
    bands = mesh.shape["band"]

    def run(spectra, endmembers, gram_inverse, abundances, duals):
        step = functools.partial(body, bands, abundances.shape[1], spectra.shape[0])
        return jax.shard_map(
            step,
            mesh=mesh,
            in_specs=(P("band", "pix"), P("band", None), P(), P(None, ("pix", "band")), P(None, ("pix", "band"))),
            out_specs=(P(None, ("pix", "band")), P(None, ("pix", "band")), P()),
            check_vma=False,
        )(spectra, endmembers, gram_inverse, abundances, duals)

    return run
```

```python
import functools

import jax
import jax.numpy as jnp
from jax import lax
from jax.experimental import pallas as pl
from jax.experimental.pallas import tpu as pltpu
from jax.sharding import PartitionSpec as P

K = 512
BISECT = 6
MESH = pl.DeviceIdType.MESH
F32 = jnp.float32
BF16 = jnp.bfloat16
SEARCH = 512
OUTER, LONG = 4, 8
OUT_PIECES = 4
PARTS = 2
VMEM_LIMIT = 24 << 20


def mxu(a, b):
    return jnp.dot(a, b, preferred_element_type=F32)


def split(value):
    high = value.astype(BF16)
    return high, (value - high.astype(F32)).astype(BF16)


def apply_model(m_high, m_low, rest):
    high, low = split(rest)
    return mxu(m_high[...], high) + mxu(m_low[...], high) + mxu(m_high[...], low)


def find_levels(shifted, levels, begin, width):
    for start in range(begin, begin + width, SEARCH):
        place = slice(start, start + SEARCH)

        def masses(*candidates):
            wide = [jnp.broadcast_to(level, (8, SEARCH)) for level in candidates]
            totals = [jnp.zeros((8, SEARCH), F32) for _ in wide]
            for k in range(0, K, 8):
                value = shifted[k:k + 8, place]
                totals = [total + jnp.maximum(value, level) for total, level in zip(totals, wide)]
            return [jnp.sum(total, axis=0, keepdims=True) - K * level for total, level in zip(totals, candidates)]

        high = total = shifted[0:8, place]
        for k in range(8, K, 8):
            value = shifted[k:k + 8, place]
            high, total = jnp.maximum(high, value), total + value
        high = jnp.max(high, axis=0, keepdims=True)
        low = (jnp.sum(total, axis=0, keepdims=True) - K) / K
        middle = 0.5 * (low + high)
        mass_low, total = masses(low, middle)
        mass_high = jnp.zeros_like(high)
        for step in range(BISECT):
            above = total > K
            low = jnp.where(above, middle, low)
            high = jnp.where(above, high, middle)
            mass_low = jnp.where(above, total, mass_low)
            mass_high = jnp.where(above, mass_high, total)
            if step < BISECT - 1:
                middle = 0.5 * (low + high)
                total, = masses(middle)
        levels[:, place] = low + (mass_low - K) * (high - low) / (mass_low - mass_high)


def lane_row(values):
    lane = lax.broadcasted_iota(jnp.int32, (1, 128), 1)
    row = jnp.zeros((1, 128), F32)
    for place, value in values:
        row = row + jnp.where(lane == place, jnp.sum(value), 0.0)
    return row


def first_kernel(bands, padded, scale, spectra, endmembers, gram_hbm, z_hbm, u_hbm,
                 y_out, e_out, m_high, m_low, shifted, levels, sums,
                 gram, z_ref, u_ref, w_high, w_low, e_send, e_recv, f_send, f_recv, y_send, y_recv, local_sem):
    me, pix = lax.axis_index("band"), lax.axis_index("pix")
    core = lax.rem(pix, 2)
    sibling = {"pix": pix + 1 - 2 * core, "band": me}
    rows = spectra.shape[0]
    columns = y_out.shape[1]
    part = columns // PARTS
    half = pl.ds(pl.multiple_of(core * (K // 2), K // 2), K // 2)

    def rows_of(band):
        return pl.ds(pl.multiple_of(band * padded, padded), rows)

    def spectra_of(band, start, width):
        return spectra.at[:, pl.ds(pl.multiple_of(band * columns + start, 128), width)]

    peers = [lax.rem(me + step, bands) for step in range(1, bands)]
    sources = [lax.rem(me + bands - step, bands) for step in range(1, bands)]
    barrier = pltpu.get_barrier_semaphore()
    for target in [{"pix": pix, "band": peer} for peer in peers] + [sibling]:
        pl.semaphore_signal(barrier, inc=1, device_id=target, device_id_type=MESH)
    own = [pltpu.make_async_copy(z_hbm, z_ref, local_sem.at[0]),
           pltpu.make_async_copy(u_hbm, u_ref, local_sem.at[1]),
           pltpu.make_async_copy(gram_hbm, gram, local_sem.at[2]),
           pltpu.make_async_copy(endmembers, e_out.at[rows_of(me), :], local_sem.at[3]),
           pltpu.make_async_copy(spectra_of(me, 0, columns), y_out.at[rows_of(me), :], local_sem.at[4])]
    for copy in own:
        copy.start()
    if padded > rows:
        for band in range(bands):
            start = band * padded + rows
            y_out[start:start + padded - rows, :] = jnp.zeros((padded - rows, columns), BF16)
            e_out[start:start + padded - rows, :] = jnp.zeros((padded - rows, K), BF16)
    pl.semaphore_wait(barrier, bands)

    copies_e = [pltpu.make_async_remote_copy(
        src_ref=endmembers.at[:, half], dst_ref=e_out.at[rows_of(me), half],
        send_sem=e_send.at[step], recv_sem=e_recv.at[step],
        device_id={"pix": pix, "band": peer}, device_id_type=MESH) for step, peer in enumerate(peers)]
    copies_y = [[pltpu.make_async_remote_copy(
        src_ref=spectra_of(peer, start, part), dst_ref=y_out.at[rows_of(me), start:start + part],
        send_sem=y_send.at[start // part, step], recv_sem=y_recv.at[start // part, step],
        device_id={"pix": pix, "band": peer}, device_id_type=MESH) for step, peer in enumerate(peers)]
        for start in range(0, columns, part)]
    for copy in sum(copies_y, copies_e):
        copy.start()
    copies_f = [pltpu.make_async_remote_copy(
        src_ref=e_out.at[rows_of(source), half], dst_ref=e_out.at[rows_of(source), half],
        send_sem=f_send.at[step], recv_sem=f_recv.at[step],
        device_id=sibling, device_id_type=MESH) for step, source in enumerate(sources)]
    for copy in own:
        copy.wait()
    for k in range(0, K, 64):
        w_high[k:k + 64, :], w_low[k:k + 64, :] = split(z_ref[k:k + 64, :] - u_ref[k:k + 64, :])
    g_high, g_low = split(gram[...])
    for start in range(0, columns, part):
        place = slice(start, start + part)
        high = w_high[:, place]
        shifted[:, place] = u_ref[:, place] + (mxu(g_high, high) + mxu(g_low, high) + mxu(g_high, w_low[:, place]))
    for arrival, copy in zip(copies_e, copies_f):
        arrival.wait_recv()
        copy.start()
    for copy in copies_f:
        copy.wait_recv()

    signatures = e_out[...]
    total = jnp.zeros((K, bands * padded), F32)
    rest = gram[...]
    for _ in range(3):
        high = rest.astype(BF16)
        total += lax.dot_general(high, signatures, (((1,), (1,)), ((), ())), preferred_element_type=F32)
        rest = rest - high.astype(F32)
    m_high[...], m_low[...] = split(total * scale)

    values = []
    for index, start in enumerate(range(0, columns, part)):
        for copy in copies_y[index]:
            copy.wait_recv()
        place = slice(start, start + part)
        arrived = y_out[:, place]
        shifted[:, place] += mxu(m_high[...], arrived) + mxu(m_low[...], arrived)
        find_levels(shifted, levels, start, part)
        level = jnp.broadcast_to(levels[:, place], (8, part))
        primal, change = jnp.zeros((8, part), F32), jnp.zeros((8, part), F32)
        for k in range(0, K, 8):
            value = shifted[k:k + 8, place]
            primal += jnp.square(jnp.minimum(value, level) - u_ref[k:k + 8, place])
            change += jnp.square(jnp.maximum(value - level, 0.0) - z_ref[k:k + 8, place])
        values += [(0, primal), (2, change)]
    sums[...] = lane_row(values)
    for copy in sum(copies_y, copies_e + copies_f):
        copy.wait_send()


def ring_distance(step, size):
    return min(step, size - step)


def second_kernel(bands, y_ref, e_ref, m_high, m_low, before, levels_before, sums_before, z_out, u_out, totals,
                  w_high, w_low, shifted, levels, mine, first, middle, second, send1, recv1, send2, recv2):
    pix, band = lax.axis_index("pix"), lax.axis_index("band")
    core, z, x = lax.rem(pix, 2), lax.rem(pix // 2, LONG), pix // (2 * LONG)
    steps1 = sorted(((dz, dc) for dz in range(LONG) for dc in range(2) if dz or dc),
                    key=lambda s: -ring_distance(s[0], LONG) * 2 - s[1])
    steps2 = sorted(((dx, dy) for dx in range(OUTER) for dy in range(bands) if dx or dy),
                    key=lambda s: -ring_distance(s[0], OUTER) - ring_distance(s[1], bands))
    targets1 = [{"pix": (x * LONG + lax.rem(z + dz, LONG)) * 2 + lax.rem(core + dc, 2), "band": band}
                for dz, dc in steps1]
    targets2 = [{"pix": (lax.rem(x + dx, OUTER) * LONG + z) * 2 + core, "band": lax.rem(band + dy, bands)}
                for dx, dy in steps2]
    barrier = pltpu.get_barrier_semaphore()
    for target in targets2 + targets1:
        pl.semaphore_signal(barrier, inc=1, device_id=target, device_id_type=MESH)

    columns = before.shape[1]
    level_before = levels_before[...]
    for k in range(0, K, 64):
        w_high[k:k + 64, :], w_low[k:k + 64, :] = split(jnp.abs(before[k:k + 64, :] - level_before) - level_before)
    modelled = (mxu(e_ref[...], w_high[...]) + mxu(e_ref[...], w_low[...])) * (1.0 / K)
    rest = y_ref[...].astype(F32) - modelled
    shifted[...] = jnp.maximum(before[...] - level_before, 0.0) + apply_model(m_high, m_low, rest)
    find_levels(shifted, levels, 0, columns)
    values = []
    for start in range(0, columns, SEARCH):
        place = slice(start, start + SEARCH)
        level = jnp.broadcast_to(levels[:, place], (8, SEARCH))
        old = jnp.broadcast_to(levels_before[:, place], (8, SEARCH))
        primal, change = jnp.zeros((8, SEARCH), F32), jnp.zeros((8, SEARCH), F32)
        for k in range(0, K, 8):
            value, earlier = shifted[k:k + 8, place], before[k:k + 8, place]
            z_new, u_new = jnp.maximum(value - level, 0.0), jnp.minimum(value, level)
            z_out[k:k + 8, place] = z_new
            u_out[k:k + 8, place] = u_new
            primal += jnp.square(u_new - jnp.minimum(earlier, old))
            change += jnp.square(z_new - jnp.maximum(earlier - old, 0.0))
        values += [(1, primal), (3, change)]
    row = sums_before[...] + lane_row(values)
    mine[...] = row
    first[0] = row
    pl.semaphore_wait(barrier, len(targets1) + len(targets2))

    def exchange(source, slots, send, recv, targets):
        for step, target in enumerate(targets):
            pltpu.make_async_remote_copy(src_ref=source, dst_ref=slots.at[step + 1], send_sem=send, recv_sem=recv,
                                         device_id=target, device_id_type=MESH).start()
        filled = slots.at[1:len(targets) + 1]
        pltpu.make_async_copy(filled, filled, recv).wait()

    exchange(mine, first, send1, recv1, targets1)
    row = jnp.sum(first[...], axis=0)
    middle[...] = row
    second[0] = row
    exchange(middle, second, send2, recv2, targets2)
    totals[...] = jnp.sum(second[...], axis=0)
    for slots, send, targets in ((first, send1, targets1), (second, send2, targets2)):
        filled = slots.at[1:len(targets) + 1]
        pltpu.make_async_copy(filled, filled, send).wait()


def last_kernel(pixels, z, u, totals, z_out, u_out, rms, sem):
    copies = []
    for piece in range(OUT_PIECES):
        rows = slice(piece * (K // OUT_PIECES), (piece + 1) * (K // OUT_PIECES))
        for which, (source, target) in enumerate(((z, z_out), (u, u_out))):
            copies.append(pltpu.make_async_copy(source.at[rows, :], target.at[rows, :], sem.at[piece, which]))
            copies[-1].start()
    row = jnp.sqrt(totals[...] / pixels)
    rms[0:1, :] = row[:, 0:2]
    rms[1:2, :] = row[:, 2:4]
    for copy in copies:
        copy.wait()


def body(bands, pixels, total_bands, spectra, endmembers, gram_inverse, abundances, duals):
    rows = spectra.shape[0]
    padded = -(-rows // 64) * 64
    depth = bands * padded
    columns = abundances.shape[1]
    penalty = total_bands / (2.0 * K * K)
    vmem = pl.BlockSpec(memory_space=pltpu.VMEM)
    hbm = pl.BlockSpec(memory_space=pltpu.HBM)
    shape = jax.ShapeDtypeStruct
    dma = pltpu.SemaphoreType.DMA
    square, wide = shape((K, columns), F32), shape((1, columns), F32)
    line = shape((1, 128), F32)
    big = pltpu.VMEM((K, columns), F32)
    packed = pltpu.VMEM((K, columns), BF16)
    y, e, m_high, m_low, shifted, levels, sums = pl.pallas_call(
        functools.partial(first_kernel, bands, padded, 1.0 / (K * penalty)),
        out_shape=(shape((depth, columns), BF16), shape((depth, K), BF16), shape((K, depth), BF16),
                   shape((K, depth), BF16), square, wide, line),
        in_specs=[hbm] * 5,
        out_specs=(vmem,) * 7,
        scratch_shapes=[pltpu.VMEM((K, K), F32), big, big, packed, packed]
        + [dma((bands - 1,))] * 4 + [dma((PARTS, bands - 1))] * 2 + [dma((5,))],
        compiler_params=pltpu.CompilerParams(collective_id=0, has_side_effects=True, vmem_limit_bytes=VMEM_LIMIT),
        name="first",
    )(*[pltpu.with_memory_space_constraint(array, pltpu.HBM)
        for array in (spectra, endmembers, gram_inverse, abundances, duals)])
    n1, n2 = 2 * LONG, OUTER * bands
    resident = pltpu.VMEM((K, columns), F32)
    z, u, totals = pl.pallas_call(
        functools.partial(second_kernel, bands),
        out_shape=(resident, resident, line),
        in_specs=[vmem] * 7,
        out_specs=(vmem,) * 3,
        scratch_shapes=[packed, packed, big, pltpu.VMEM((1, columns), F32), pltpu.VMEM((1, 128), F32),
                        pltpu.VMEM((n1, 1, 128), F32), pltpu.VMEM((1, 128), F32), pltpu.VMEM((n2, 1, 128), F32)]
        + [dma] * 4,
        compiler_params=pltpu.CompilerParams(collective_id=1, has_side_effects=True, vmem_limit_bytes=VMEM_LIMIT),
        name="second",
    )(y, e, m_high, m_low, shifted, levels, sums)
    return pl.pallas_call(
        functools.partial(last_kernel, pixels),
        out_shape=(square, square, shape((2, 2), F32)),
        in_specs=[vmem] * 3,
        out_specs=(hbm, hbm, vmem),
        scratch_shapes=[dma((OUT_PIECES, 2))],
        compiler_params=pltpu.CompilerParams(vmem_limit_bytes=VMEM_LIMIT),
        name="last",
    )(z, u, totals)


def solution(mesh):
    bands = mesh.shape["band"]

    def run(spectra, endmembers, gram_inverse, abundances, duals):
        step = functools.partial(body, bands, abundances.shape[1], spectra.shape[0])
        return jax.shard_map(
            step,
            mesh=mesh,
            in_specs=(P("band", "pix"), P("band", None), P(), P(None, ("pix", "band")), P(None, ("pix", "band"))),
            out_specs=(P(None, ("pix", "band")), P(None, ("pix", "band")), P()),
            check_vma=False,
        )(spectra, endmembers, gram_inverse, abundances, duals)

    return run
```

```python
import functools

import jax
import jax.numpy as jnp
from jax import lax
from jax.experimental import pallas as pl
from jax.experimental.pallas import tpu as pltpu
from jax.sharding import PartitionSpec as P

K = 512
BISECT = 6
MESH = pl.DeviceIdType.MESH
F32 = jnp.float32
BF16 = jnp.bfloat16
SEARCH = 512
OUTER, LONG = 4, 8
OUT_PIECES = 4
PARTS = 2
VMEM_LIMIT = 24 << 20


def mxu(a, b):
    return jnp.dot(a, b, preferred_element_type=F32)


def split(value):
    high = value.astype(BF16)
    return high, (value - high.astype(F32)).astype(BF16)


def apply_model(m_high, m_low, rest):
    high, low = split(rest)
    return mxu(m_high[...], high) + mxu(m_low[...], high) + mxu(m_high[...], low)


def find_levels(shifted, levels, begin, width):
    places = [slice(start, start + SEARCH) for start in range(begin, begin + width, SEARCH)]

    def masses(place, *candidates):
        wide = [jnp.broadcast_to(level, (8, SEARCH)) for level in candidates]
        totals = [jnp.zeros((8, SEARCH), F32) for _ in wide]
        for k in range(0, K, 8):
            value = shifted[k:k + 8, place]
            totals = [total + jnp.maximum(value, level) for total, level in zip(totals, wide)]
        return [jnp.sum(total, axis=0, keepdims=True) - K * level for total, level in zip(totals, candidates)]

    states = []
    for place in places:
        high = total = shifted[0:8, place]
        for k in range(8, K, 8):
            value = shifted[k:k + 8, place]
            high, total = jnp.maximum(high, value), total + value
        high = jnp.max(high, axis=0, keepdims=True)
        low = (jnp.sum(total, axis=0, keepdims=True) - K) / K
        states.append((low, high, None, jnp.zeros_like(high)))
    for step in range(BISECT):
        for index, (place, (low, high, mass_low, mass_high)) in enumerate(zip(places, states)):
            middle = 0.5 * (low + high)
            if step == 0:
                mass_low, total = masses(place, low, middle)
            else:
                total, = masses(place, middle)
            above = total > K
            states[index] = (jnp.where(above, middle, low), jnp.where(above, high, middle),
                             jnp.where(above, total, mass_low), jnp.where(above, mass_high, total))
    for place, (low, high, mass_low, mass_high) in zip(places, states):
        levels[:, place] = low + (mass_low - K) * (high - low) / (mass_low - mass_high)


def lane_row(values):
    lane = lax.broadcasted_iota(jnp.int32, (1, 128), 1)
    row = jnp.zeros((1, 128), F32)
    for place, value in values:
        row = row + jnp.where(lane == place, jnp.sum(value), 0.0)
    return row


def first_kernel(bands, padded, scale, spectra, endmembers, gram_hbm, z_hbm, u_hbm,
                 y_out, e_out, m_high, m_low, shifted, levels, sums,
                 gram, z_ref, u_ref, w_high, w_low, e_send, e_recv, f_send, f_recv, y_send, y_recv, local_sem):
    me, pix = lax.axis_index("band"), lax.axis_index("pix")
    core = lax.rem(pix, 2)
    sibling = {"pix": pix + 1 - 2 * core, "band": me}
    rows = spectra.shape[0]
    columns = y_out.shape[1]
    part = columns // PARTS
    half = pl.ds(pl.multiple_of(core * (K // 2), K // 2), K // 2)

    def rows_of(band):
        return pl.ds(pl.multiple_of(band * padded, padded), rows)

    def spectra_of(band, start, width):
        return spectra.at[:, pl.ds(pl.multiple_of(band * columns + start, 128), width)]

    peers = [lax.rem(me + step, bands) for step in range(1, bands)]
    sources = [lax.rem(me + bands - step, bands) for step in range(1, bands)]
    barrier = pltpu.get_barrier_semaphore()
    for target in [{"pix": pix, "band": peer} for peer in peers] + [sibling]:
        pl.semaphore_signal(barrier, inc=1, device_id=target, device_id_type=MESH)
    own = [pltpu.make_async_copy(z_hbm, z_ref, local_sem.at[0]),
           pltpu.make_async_copy(u_hbm, u_ref, local_sem.at[1]),
           pltpu.make_async_copy(gram_hbm, gram, local_sem.at[2]),
           pltpu.make_async_copy(endmembers, e_out.at[rows_of(me), :], local_sem.at[3]),
           pltpu.make_async_copy(spectra_of(me, 0, columns), y_out.at[rows_of(me), :], local_sem.at[4])]
    for copy in own:
        copy.start()
    if padded > rows:
        for band in range(bands):
            start = band * padded + rows
            y_out[start:start + padded - rows, :] = jnp.zeros((padded - rows, columns), BF16)
            e_out[start:start + padded - rows, :] = jnp.zeros((padded - rows, K), BF16)
    pl.semaphore_wait(barrier, bands)

    copies_e = [pltpu.make_async_remote_copy(
        src_ref=endmembers.at[:, half], dst_ref=e_out.at[rows_of(me), half],
        send_sem=e_send.at[step], recv_sem=e_recv.at[step],
        device_id={"pix": pix, "band": peer}, device_id_type=MESH) for step, peer in enumerate(peers)]
    copies_y = [[pltpu.make_async_remote_copy(
        src_ref=spectra_of(peer, start, part), dst_ref=y_out.at[rows_of(me), start:start + part],
        send_sem=y_send.at[start // part, step], recv_sem=y_recv.at[start // part, step],
        device_id={"pix": pix, "band": peer}, device_id_type=MESH) for step, peer in enumerate(peers)]
        for start in range(0, columns, part)]
    for copy in sum(copies_y, copies_e):
        copy.start()
    copies_f = [pltpu.make_async_remote_copy(
        src_ref=e_out.at[rows_of(source), half], dst_ref=e_out.at[rows_of(source), half],
        send_sem=f_send.at[step], recv_sem=f_recv.at[step],
        device_id=sibling, device_id_type=MESH) for step, source in enumerate(sources)]
    for copy in own:
        copy.wait()
    for k in range(0, K, 64):
        w_high[k:k + 64, :], w_low[k:k + 64, :] = split(z_ref[k:k + 64, :] - u_ref[k:k + 64, :])
    g_high, g_low = split(gram[...])
    for start in range(0, columns, part):
        place = slice(start, start + part)
        high = w_high[:, place]
        shifted[:, place] = u_ref[:, place] + (mxu(g_high, high) + mxu(g_low, high) + mxu(g_high, w_low[:, place]))
    for arrival, copy in zip(copies_e, copies_f):
        arrival.wait_recv()
        copy.start()
    for copy in copies_f:
        copy.wait_recv()

    signatures = e_out[...]
    total = jnp.zeros((K, bands * padded), F32)
    rest = gram[...]
    for _ in range(3):
        high = rest.astype(BF16)
        total += lax.dot_general(high, signatures, (((1,), (1,)), ((), ())), preferred_element_type=F32)
        rest = rest - high.astype(F32)
    m_high[...], m_low[...] = split(total * scale)

    values = []
    for index, start in enumerate(range(0, columns, part)):
        for copy in copies_y[index]:
            copy.wait_recv()
        place = slice(start, start + part)
        arrived = y_out[:, place]
        shifted[:, place] += mxu(m_high[...], arrived) + mxu(m_low[...], arrived)
        find_levels(shifted, levels, start, part)
        level = jnp.broadcast_to(levels[:, place], (8, part))
        primal, change = jnp.zeros((8, part), F32), jnp.zeros((8, part), F32)
        for k in range(0, K, 8):
            value = shifted[k:k + 8, place]
            primal += jnp.square(jnp.minimum(value, level) - u_ref[k:k + 8, place])
            change += jnp.square(jnp.maximum(value - level, 0.0) - z_ref[k:k + 8, place])
        values += [(0, primal), (2, change)]
    sums[...] = lane_row(values)
    for copy in sum(copies_y, copies_e + copies_f):
        copy.wait_send()


def ring_distance(step, size):
    return min(step, size - step)


def second_kernel(bands, y_ref, e_ref, m_high, m_low, before, levels_before, sums_before, z_out, u_out, totals,
                  w_high, w_low, shifted, levels, mine, first, middle, second, send1, recv1, send2, recv2):
    pix, band = lax.axis_index("pix"), lax.axis_index("band")
    core, z, x = lax.rem(pix, 2), lax.rem(pix // 2, LONG), pix // (2 * LONG)
    steps1 = sorted(((dz, dc) for dz in range(LONG) for dc in range(2) if dz or dc),
                    key=lambda s: -ring_distance(s[0], LONG) * 2 - s[1])
    steps2 = sorted(((dx, dy) for dx in range(OUTER) for dy in range(bands) if dx or dy),
                    key=lambda s: -ring_distance(s[0], OUTER) - ring_distance(s[1], bands))
    targets1 = [{"pix": (x * LONG + lax.rem(z + dz, LONG)) * 2 + lax.rem(core + dc, 2), "band": band}
                for dz, dc in steps1]
    targets2 = [{"pix": (lax.rem(x + dx, OUTER) * LONG + z) * 2 + core, "band": lax.rem(band + dy, bands)}
                for dx, dy in steps2]
    barrier = pltpu.get_barrier_semaphore()
    for target in targets2 + targets1:
        pl.semaphore_signal(barrier, inc=1, device_id=target, device_id_type=MESH)

    columns = before.shape[1]
    level_before = levels_before[...]
    for k in range(0, K, 64):
        w_high[k:k + 64, :], w_low[k:k + 64, :] = split(jnp.abs(before[k:k + 64, :] - level_before) - level_before)
    modelled = (mxu(e_ref[...], w_high[...]) + mxu(e_ref[...], w_low[...])) * (1.0 / K)
    rest = y_ref[...].astype(F32) - modelled
    shifted[...] = jnp.maximum(before[...] - level_before, 0.0) + apply_model(m_high, m_low, rest)
    find_levels(shifted, levels, 0, columns)
    values = []
    for start in range(0, columns, SEARCH):
        place = slice(start, start + SEARCH)
        level = jnp.broadcast_to(levels[:, place], (8, SEARCH))
        old = jnp.broadcast_to(levels_before[:, place], (8, SEARCH))
        primal, change = jnp.zeros((8, SEARCH), F32), jnp.zeros((8, SEARCH), F32)
        for k in range(0, K, 8):
            value, earlier = shifted[k:k + 8, place], before[k:k + 8, place]
            z_new, u_new = jnp.maximum(value - level, 0.0), jnp.minimum(value, level)
            z_out[k:k + 8, place] = z_new
            u_out[k:k + 8, place] = u_new
            primal += jnp.square(u_new - jnp.minimum(earlier, old))
            change += jnp.square(z_new - jnp.maximum(earlier - old, 0.0))
        values += [(1, primal), (3, change)]
    row = sums_before[...] + lane_row(values)
    mine[...] = row
    first[0] = row
    pl.semaphore_wait(barrier, len(targets1) + len(targets2))

    def exchange(source, slots, send, recv, targets):
        for step, target in enumerate(targets):
            pltpu.make_async_remote_copy(src_ref=source, dst_ref=slots.at[step + 1], send_sem=send, recv_sem=recv,
                                         device_id=target, device_id_type=MESH).start()
        filled = slots.at[1:len(targets) + 1]
        pltpu.make_async_copy(filled, filled, recv).wait()

    exchange(mine, first, send1, recv1, targets1)
    row = jnp.sum(first[...], axis=0)
    middle[...] = row
    second[0] = row
    exchange(middle, second, send2, recv2, targets2)
    totals[...] = jnp.sum(second[...], axis=0)
    for slots, send, targets in ((first, send1, targets1), (second, send2, targets2)):
        filled = slots.at[1:len(targets) + 1]
        pltpu.make_async_copy(filled, filled, send).wait()


def last_kernel(pixels, z, u, totals, z_out, u_out, rms, sem):
    copies = []
    for piece in range(OUT_PIECES):
        rows = slice(piece * (K // OUT_PIECES), (piece + 1) * (K // OUT_PIECES))
        for which, (source, target) in enumerate(((z, z_out), (u, u_out))):
            copies.append(pltpu.make_async_copy(source.at[rows, :], target.at[rows, :], sem.at[piece, which]))
            copies[-1].start()
    row = jnp.sqrt(totals[...] / pixels)
    rms[0:1, :] = row[:, 0:2]
    rms[1:2, :] = row[:, 2:4]
    for copy in copies:
        copy.wait()


def body(bands, pixels, total_bands, spectra, endmembers, gram_inverse, abundances, duals):
    rows = spectra.shape[0]
    padded = -(-rows // 64) * 64
    depth = bands * padded
    columns = abundances.shape[1]
    penalty = total_bands / (2.0 * K * K)
    vmem = pl.BlockSpec(memory_space=pltpu.VMEM)
    hbm = pl.BlockSpec(memory_space=pltpu.HBM)
    shape = jax.ShapeDtypeStruct
    dma = pltpu.SemaphoreType.DMA
    square, wide = shape((K, columns), F32), shape((1, columns), F32)
    line = shape((1, 128), F32)
    big = pltpu.VMEM((K, columns), F32)
    packed = pltpu.VMEM((K, columns), BF16)
    y, e, m_high, m_low, shifted, levels, sums = pl.pallas_call(
        functools.partial(first_kernel, bands, padded, 1.0 / (K * penalty)),
        out_shape=(shape((depth, columns), BF16), shape((depth, K), BF16), shape((K, depth), BF16),
                   shape((K, depth), BF16), square, wide, line),
        in_specs=[hbm] * 5,
        out_specs=(vmem,) * 7,
        scratch_shapes=[pltpu.VMEM((K, K), F32), big, big, packed, packed]
        + [dma((bands - 1,))] * 4 + [dma((PARTS, bands - 1))] * 2 + [dma((5,))],
        compiler_params=pltpu.CompilerParams(collective_id=0, has_side_effects=True, vmem_limit_bytes=VMEM_LIMIT),
        name="first",
    )(*[pltpu.with_memory_space_constraint(array, pltpu.HBM)
        for array in (spectra, endmembers, gram_inverse, abundances, duals)])
    n1, n2 = 2 * LONG, OUTER * bands
    resident = pltpu.VMEM((K, columns), F32)
    z, u, totals = pl.pallas_call(
        functools.partial(second_kernel, bands),
        out_shape=(resident, resident, line),
        in_specs=[vmem] * 7,
        out_specs=(vmem,) * 3,
        scratch_shapes=[packed, packed, big, pltpu.VMEM((1, columns), F32), pltpu.VMEM((1, 128), F32),
                        pltpu.VMEM((n1, 1, 128), F32), pltpu.VMEM((1, 128), F32), pltpu.VMEM((n2, 1, 128), F32)]
        + [dma] * 4,
        compiler_params=pltpu.CompilerParams(collective_id=1, has_side_effects=True, vmem_limit_bytes=VMEM_LIMIT),
        name="second",
    )(y, e, m_high, m_low, shifted, levels, sums)
    return pl.pallas_call(
        functools.partial(last_kernel, pixels),
        out_shape=(square, square, shape((2, 2), F32)),
        in_specs=[vmem] * 3,
        out_specs=(hbm, hbm, vmem),
        scratch_shapes=[dma((OUT_PIECES, 2))],
        compiler_params=pltpu.CompilerParams(vmem_limit_bytes=VMEM_LIMIT),
        name="last",
    )(z, u, totals)


def solution(mesh):
    bands = mesh.shape["band"]

    def run(spectra, endmembers, gram_inverse, abundances, duals):
        step = functools.partial(body, bands, abundances.shape[1], spectra.shape[0])
        return jax.shard_map(
            step,
            mesh=mesh,
            in_specs=(P("band", "pix"), P("band", None), P(), P(None, ("pix", "band")), P(None, ("pix", "band"))),
            out_specs=(P(None, ("pix", "band")), P(None, ("pix", "band")), P()),
            check_vma=False,
        )(spectra, endmembers, gram_inverse, abundances, duals)

    return run
```
